32 devices in a mesh: groups: 2 (over y), ctx: 4 (over z), head: 4 (over x, core).
Axes of the slice: x: 2, y: 2, z: 4, core: 2. Of those that a mesh axis runs over, the one named last changes fastest.
Arguments:
- queries: bfloat16 [64, 2048, 128], P(('groups', 'head'), 'ctx'), parts along dimension 0, may hold values from -48 to 48
- key_rows: bfloat16 [8, 2048, 128], P(('groups', 'head'), 'ctx'), parts along dimension 0, may hold values from -6 to 6
- value_rows: bfloat16 [8, 2048, 128], P(('groups', 'head'), 'ctx'), parts along dimension 0, may hold values from -6 to 6
- out_grad: bfloat16 [64, 2048, 128], P(('groups', 'head'), 'ctx'), parts along dimension 0, may hold values from -6 to 6
- link_mask: int32 [32, 11], P(('groups', 'ctx')), parts along dimension 0, may hold values from 0 to 1, as said below
Outputs:
- output: bfloat16 [64, 2048, 128], P(('groups', 'head'), 'ctx'), parts along dimension 0
- query_grad: bfloat16 [64, 2048, 128], P(('groups', 'head'), 'ctx'), parts along dimension 0
- key_grad: bfloat16 [8, 2048, 128], P(('groups', 'head'), 'ctx'), parts along dimension 0
- value_grad: bfloat16 [8, 2048, 128], P(('groups', 'head'), 'ctx'), parts along dimension 0
The draws below stay inside these ranges and needn't reach their ends.
There are 2 independent parts, one for each index of `groups`. The reference program is written for one: setup_inputs(seed, part) draws one part's arguments, and reference() takes and returns one part's arrays. A program takes and returns all parts, laid end to end along the dimension named above; each array names one. Nothing has to cross between parts.
Inputs may be any that keep to these rules, and one draw needn't show every extreme that they name: `link_mask`: column 0 is 1 in every row.
All inputs are finite; a program needn't handle non-finite values.
Results may differ from the reference program's by a relative error of at most 0.028.
Values may be sent and summed in bfloat16 or wider, within the bound.
No kernel may reach another device: no remote copies, remote signals or barrier semaphores. Data moves between devices by JAX's collectives and lax.ppermute only.
A program may use at most 64 MiB of HBM per device.

```python
import math
import jax
import jax.numpy as jnp
from jax import lax

HEADS = 8
HD = 128
BLK = 128
NOFF = 11
KVG = 4
SEQ = 2048


def drawn_pair(key):
    key_query, key_keys = jax.random.split(key, 2)
    total_heads = KVG * HEADS
    query_draw = jnp.clip(1.5 * jax.random.normal(key_query, (total_heads, SEQ, HD), jnp.float32), -9.0, 9.0)
    key_draw = jnp.clip(jax.random.normal(key_keys, (KVG, SEQ, HD), jnp.float32), -6.0, 6.0)
    return (query_draw, key_draw)


def draw_queries(key, part):
    return drawn_pair(jax.random.fold_in(key, 11))[0].astype(jnp.bfloat16)


def draw_key_rows(key, part):
    return drawn_pair(jax.random.fold_in(key, 11))[1].astype(jnp.bfloat16)


def draw_link_mask(key, part):
    levels = jax.random.randint(jax.random.fold_in(key, 23), (SEQ // BLK, NOFF), 0, 4)
    kept = (levels > 0).astype(jnp.int32)
    return kept.at[:, 0].set(1)


def level_of(own_key, shape, cuts, least, largest):
    def one(position, parts):
        heights = jax.random.uniform(jax.random.fold_in(jax.random.fold_in(own_key, 6), position), (parts,), jnp.float32, least / len(cuts), largest / len(cuts))
        return jnp.repeat(jnp.exp(heights), shape[position] // parts).reshape((-1,) + (1,) * (len(shape) - position - 1))

    loudness = one(*cuts[0])
    for cut in cuts[1:]:
        loudness = loudness * one(*cut)
    return loudness


def noise(stream_key, dims, width, bound, cuts=(), kind=jnp.bfloat16):
    entries = jax.random.normal(stream_key, dims, jnp.float32) * width
    if len(cuts) > 0:
        entries = level_of(stream_key, dims, cuts, -0.22, 0.18) * entries
    return jnp.clip(entries, min=-bound, max=bound).astype(kind)


def setup_inputs(seed: int = 0, part: int = 0) -> dict:
    keys = jax.random.split(jax.random.key(seed), 6)
    part_splits = jax.random.split(jax.random.fold_in(keys[5], part), 6)
    return {
        "queries": draw_queries(jax.random.fold_in(jax.random.fold_in(keys[5], part), 71), part),
        "key_rows": draw_key_rows(jax.random.fold_in(jax.random.fold_in(keys[5], part), 71), part),
        "value_rows": noise(part_splits[2], (KVG, SEQ, HD), 1.0, 6.0, ((0, 4), (1, 4))),
        "out_grad": noise(part_splits[3], (KVG * HEADS, SEQ, HD), 1.0, 6.0, ((0, 4), (1, 4))),
        "link_mask": draw_link_mask(jax.random.fold_in(jax.random.fold_in(keys[5], part), 71), part),
    }


def one_group(queries, key_rows, value_rows, out_grad, link_mask):
    block_total = SEQ // BLK
    inv_root = 1.0 / math.sqrt(HD)
    offsets = jnp.array([0] + [2 ** slot for slot in range(NOFF - 1)], dtype=jnp.int32)
    query_blocks = queries.reshape(HEADS, block_total, BLK, HD)
    grad_blocks = out_grad.reshape(HEADS, block_total, BLK, HD)
    key_blocks = key_rows.reshape(block_total, BLK, HD)
    value_blocks = value_rows.reshape(block_total, BLK, HD)
    causal = jnp.arange(BLK)[None, :] <= jnp.arange(BLK)[:, None]
    is_diagonal = jnp.arange(NOFF) == 0

    def block_step(running, block_id):
        key_acc, value_acc = running
        source = (block_id - offsets).astype(jnp.int32)
        link_live = (source >= 0) & (link_mask[block_id] == 1)
        source = jnp.maximum(source, 0).astype(jnp.int32)
        key_part = key_blocks[source].astype(jnp.float32)
        value_part = value_blocks[source].astype(jnp.float32)
        query_part = lax.dynamic_index_in_dim(query_blocks, block_id, 1, keepdims=False).astype(jnp.float32)
        grad_part = lax.dynamic_index_in_dim(grad_blocks, block_id, 1, keepdims=False).astype(jnp.float32)
        allowed = link_live[None, :, None] & (causal[:, None, :] | (~is_diagonal)[None, :, None])
        scores = jnp.einsum('htd,jud->htju', query_part, key_part) * inv_root
        scores = jnp.where(allowed[None], scores, -jnp.inf)
        row_max = lax.optimization_barrier(jnp.max(scores, axis=(2, 3), keepdims=True))
        log_total = row_max + jnp.log(lax.optimization_barrier(jnp.sum(jnp.exp(scores - row_max), axis=(2, 3), keepdims=True)))
        weights = jnp.exp(scores - log_total)
        weights_low = lax.optimization_barrier(weights.astype(jnp.bfloat16)).astype(jnp.float32)
        output = jnp.einsum('htju,jud->htd', weights_low, value_part).astype(jnp.bfloat16)
        row_dot = lax.optimization_barrier(jnp.sum(grad_part * output.astype(jnp.float32), axis=-1))[:, :, None, None]
        grad_weights = jnp.einsum('htd,jud->htju', grad_part, value_part)
        grad_scores = weights * (grad_weights - row_dot) * inv_root
        grad_scores = lax.optimization_barrier(grad_scores.astype(jnp.bfloat16)).astype(jnp.float32)
        query_grad = jnp.einsum('htju,jud->htd', grad_scores, key_part).astype(jnp.bfloat16)
        key_part_grad = jnp.einsum('htju,htd->jud', grad_scores, query_part)
        value_part_grad = jnp.einsum('htju,htd->jud', weights_low, grad_part)
        key_acc = key_acc.at[source].add(key_part_grad)
        value_acc = value_acc.at[source].add(value_part_grad)
        return ((key_acc, value_acc), (output, query_grad))
    empty = jnp.zeros((block_total, BLK, HD), jnp.float32)
    (key_acc, value_acc), (outputs, query_grads) = lax.scan(block_step, (empty, empty), jnp.arange(block_total, dtype=jnp.int32))
    output = jnp.transpose(outputs, (1, 0, 2, 3)).reshape(HEADS, SEQ, HD)
    query_grad = jnp.transpose(query_grads, (1, 0, 2, 3)).reshape(HEADS, SEQ, HD)
    key_grad = key_acc.reshape(SEQ, HD).astype(jnp.bfloat16)
    value_grad = value_acc.reshape(SEQ, HD).astype(jnp.bfloat16)
    return (output, query_grad, key_grad, value_grad)

def reference(queries, key_rows, value_rows, out_grad, link_mask):
    grouped_q = queries.reshape(KVG, HEADS, SEQ, HD)
    grouped_g = out_grad.reshape(KVG, HEADS, SEQ, HD)

    def run(items):
        return one_group(items[0], items[1], items[2], items[3], link_mask)
    output, query_grad, key_grad, value_grad = lax.map(run, (grouped_q, key_rows, value_rows, grouped_g))
    return (output.reshape(KVG * HEADS, SEQ, HD), query_grad.reshape(KVG * HEADS, SEQ, HD), key_grad, value_grad)
```

```python
import functools
import math

import jax
import jax.numpy as jnp
from jax import lax
from jax.experimental import pallas as pl
from jax.experimental.pallas import tpu as pltpu
from jax.sharding import PartitionSpec as P

BLK = 128
NOFF = 11
NEG = -1e30
LOG2E = 1.4426950408889634
F32 = jnp.float32
BF16 = jnp.bfloat16


def shift(value, axis, steps):
    count = lax.axis_size(axis)
    first, last = (max(0, -steps), min(count, count - steps))
    return lax.ppermute(value, axis, [(source, source + steps) for source in range(first, last)])


def slot_table(block_count, ctx_size):
    entries = []
    for slot_id in range(NOFF):
        offset = 0 if slot_id == 0 else 2 ** (slot_id - 1)
        if offset < block_count:
            entries.append((slot_id, offset, 0))
        elif offset // block_count < ctx_size:
            entries.append((slot_id, offset, offset // block_count))
    return entries


def dot_nt(a, b):
    return lax.dot_general(a, b, (((1,), (1,)), ((), ())), preferred_element_type=F32)


def dot_nn(a, b):
    return lax.dot_general(a, b, (((1,), (0,)), ((), ())), preferred_element_type=F32)


def causal(width):
    key = lax.broadcasted_iota(jnp.int32, (BLK, width), 0)
    row = lax.broadcasted_iota(jnp.int32, (BLK, width), 1)
    return key <= lax.rem(row, BLK)


def bias_of(live_ref, step, entry):
    return jnp.where(live_ref[step, entry] == 1, 0.0, NEG).astype(F32)


def near_start(step, offset, block_count):
    return pl.multiple_of((step + block_count - offset) * BLK, BLK)


def near_forward(near, pairs, live_ref, q_ref, k_ref, v_ref, kp_ref, vp_ref, stat_ref, acc_ref, kcat, vtcat):
    step = pl.program_id(0)
    rows = k_ref.shape[0]
    blocks = rows // BLK
    size = k_ref.shape[1]
    scale = LOG2E / math.sqrt(size)

    @pl.when(step == 0)
    def _():
        kcat[:rows] = kp_ref[...]
        kcat[rows:] = k_ref[...]
        vtcat[:, :rows] = vp_ref[...].T
        vtcat[:, rows:] = v_ref[...].T

    starts = [near_start(step, offset, blocks) for _, (_, offset, _) in near]
    keys = jnp.concatenate([kcat[pl.ds(start, BLK), :] for start in starts], axis=0)
    values_t = jnp.concatenate([vtcat[:, pl.ds(start, BLK)] for start in starts], axis=1)
    biases = [bias_of(live_ref, step, entry) for entry, _ in near]
    heads = q_ref.shape[0]
    wide = pairs * BLK
    mask = causal(wide)
    for first in range(0, heads, pairs):
        lanes = slice(first * BLK, first * BLK + wide)
        q = q_ref[first : first + pairs].reshape(wide, size)
        scores = dot_nt(keys, q) * scale
        parts = [scores[n * BLK : (n + 1) * BLK] for n in range(len(near))]
        parts[0] = jnp.where(mask, parts[0], NEG)
        top = None
        for part, bias in zip(parts, biases):
            part_top = jnp.max(part, axis=0, keepdims=True) + bias
            top = part_top if top is None else jnp.maximum(top, part_top)
        exps = [jnp.exp2(part - (top - bias)) for part, bias in zip(parts, biases)]
        total = sum(jnp.sum(part, axis=0, keepdims=True) for part in exps)
        low = jnp.concatenate([part.astype(BF16) for part in exps], axis=0)
        stat_ref[0, 0:1, lanes] = top
        stat_ref[0, 1:2, lanes] = total
        acc_ref[0, :, lanes] = dot_nn(values_t, low)


def far_both(far, pairs, live_ref, q_ref, do_ref, kf_ref, vf_ref, stat_ref, acc_ref, o_ref, dkf_ref, dvf_ref, ds_ref, fin_ref):
    step = pl.program_id(0)
    count = len(far)
    heads, _, size = q_ref.shape
    inv_root = 1.0 / math.sqrt(size)
    scale = LOG2E * inv_root
    keys = kf_ref[...].reshape(count * BLK, size)
    values = vf_ref[...].reshape(count * BLK, size)
    values_t = values.T
    biases = [bias_of(live_ref, step, entry) for entry, _ in far]
    wide = pairs * BLK
    dk = jnp.zeros((count * BLK, size), F32)
    dv = jnp.zeros((count * BLK, size), F32)
    for first in range(0, heads, pairs):
        lanes = slice(first * BLK, first * BLK + wide)
        q = q_ref[first : first + pairs].reshape(wide, size)
        do = do_ref[first : first + pairs].reshape(wide, size)
        scores = dot_nt(keys, q) * scale
        grad_w = dot_nt(values, do)
        parts = [scores[n * BLK : (n + 1) * BLK] for n in range(count)]
        near_top = stat_ref[0, 0:1, lanes]
        top = near_top
        for part, bias in zip(parts, biases):
            top = jnp.maximum(top, jnp.max(part, axis=0, keepdims=True) + bias)
        exps = [jnp.exp2(part - (top - bias)) for part, bias in zip(parts, biases)]
        fade = jnp.exp2(near_top - top)
        total = stat_ref[0, 1:2, lanes] * fade
        total = total + sum(jnp.sum(part, axis=0, keepdims=True) for part in exps)
        inverse = 1.0 / total
        weights = jnp.concatenate(exps, axis=0) * inverse
        low = weights.astype(BF16)
        out_t = acc_ref[0, :, lanes] * (fade * inverse) + dot_nn(values_t, low)
        out_low_t = out_t.astype(BF16)
        o_ref[first : first + pairs] = out_low_t.T.reshape(pairs, BLK, size)
        row_dot = jnp.sum(out_low_t.astype(F32) * do.T.astype(F32), axis=0, keepdims=True)
        ds = (weights * (grad_w - row_dot)).astype(BF16)
        ds_ref[0, :, lanes] = ds
        fin_ref[0, 0:1, lanes] = top + jnp.log2(total)
        fin_ref[0, 1:2, lanes] = row_dot
        dk += dot_nn(ds, q)
        dv += dot_nn(low, do)
    dkf_ref[...] = (dk * inv_root).astype(BF16).reshape(dkf_ref.shape)
    dvf_ref[...] = dv.astype(BF16).reshape(dvf_ref.shape)


def near_backward(
    near, pairs, live_ref, q_ref, do_ref, k_ref, v_ref, kp_ref, vp_ref, kf_ref, fin_ref, ds_ref,
    dq_ref, dk_ref, dv_ref, dkp_ref, dvp_ref, kcat, vcat, dkcat, dvcat
):
    step = pl.program_id(0)
    rows = k_ref.shape[0]
    blocks = rows // BLK
    heads, _, size = q_ref.shape
    inv_root = 1.0 / math.sqrt(size)
    scale = LOG2E * inv_root

    @pl.when(step == 0)
    def _():
        kcat[:rows] = kp_ref[...]
        kcat[rows:] = k_ref[...]
        vcat[:rows] = vp_ref[...]
        vcat[rows:] = v_ref[...]
        dkcat[...] = jnp.zeros_like(dkcat)
        dvcat[...] = jnp.zeros_like(dvcat)

    starts = [near_start(step, offset, blocks) for _, (_, offset, _) in near]
    keys = jnp.concatenate([kcat[pl.ds(start, BLK), :] for start in starts], axis=0)
    values = jnp.concatenate([vcat[pl.ds(start, BLK), :] for start in starts], axis=0)
    far_count = kf_ref.shape[0]
    all_keys_t = jnp.concatenate([keys, kf_ref[...].reshape(far_count * BLK, size)], axis=0).T
    biases = [bias_of(live_ref, step, entry) for entry, _ in near]
    wide = pairs * BLK
    mask = causal(wide)
    dk = jnp.zeros((len(near) * BLK, size), F32)
    dv = jnp.zeros((len(near) * BLK, size), F32)
    for first in range(0, heads, pairs):
        lanes = slice(first * BLK, first * BLK + wide)
        q = q_ref[first : first + pairs].reshape(wide, size)
        do = do_ref[first : first + pairs].reshape(wide, size)
        scores = dot_nt(keys, q) * scale
        grad_w = dot_nt(values, do)
        log_total = fin_ref[0, 0:1, lanes]
        row_dot = fin_ref[0, 1:2, lanes]
        parts = [scores[n * BLK : (n + 1) * BLK] for n in range(len(near))]
        parts[0] = jnp.where(mask, parts[0], NEG)
        weights = jnp.concatenate(
            [jnp.exp2(part - (log_total - bias)) for part, bias in zip(parts, biases)], axis=0
        )
        ds = (weights * (grad_w - row_dot)).astype(BF16)
        low = weights.astype(BF16)
        dk += dot_nn(ds, q)
        dv += dot_nn(low, do)
        all_ds = jnp.concatenate([ds, ds_ref[0, :, lanes]], axis=0)
        dq_t = (dot_nn(all_keys_t, all_ds) * inv_root).astype(BF16)
        dq_ref[first : first + pairs] = dq_t.T.reshape(pairs, BLK, size)
    for n, start in enumerate(starts):
        dkcat[pl.ds(start, BLK), :] += dk[n * BLK : (n + 1) * BLK]
        dvcat[pl.ds(start, BLK), :] += dv[n * BLK : (n + 1) * BLK]

    @pl.when(step == blocks - 1)
    def _():
        dkp_ref[...] = dkcat[:rows] * inv_root
        dk_ref[...] = dkcat[rows:] * inv_root
        dvp_ref[...] = dvcat[:rows]
        dv_ref[...] = dvcat[rows:]


def local(queries, key_rows, value_rows, out_grad, link_mask):
    heads, rows, size = queries.shape
    blocks = rows // BLK
    ctx_size = lax.axis_size("ctx")
    entries = slot_table(blocks, ctx_size)
    near = [(n, e) for n, e in enumerate(entries) if e[1] <= blocks]
    far = [(n, e) for n, e in enumerate(entries) if e[1] > blocks]
    hops = [e[2] for _, e in far]
    pairs = 2

    keys, values = key_rows[0], value_rows[0]
    with jax.named_scope("hop_k1"):
        k_prev = shift(keys, "ctx", 1)
    with jax.named_scope("hop_v1"):
        v_prev = shift(values, "ctx", 1)
    k_far, v_far = [], []
    k_last, v_last, at = k_prev, v_prev, 1
    for hop in hops:
        with jax.named_scope(f"hop_k{hop}"):
            k_last = shift(k_last, "ctx", hop - at)
        with jax.named_scope(f"hop_v{hop}"):
            v_last = shift(v_last, "ctx", hop - at)
        at = hop
        k_far.append(k_last)
        v_far.append(v_last)
    if len(far) == 1:
        k_far, v_far = k_far[0][None], v_far[0][None]
    else:
        k_far, v_far = jnp.stack(k_far), jnp.stack(v_far)

    block_ids = lax.axis_index("ctx") * blocks + jnp.arange(blocks)
    slot_ids = jnp.array([e[0] for e in entries])
    offsets = jnp.array([e[1] for e in entries])
    live = (link_mask[:, slot_ids] == 1) & (block_ids[:, None] >= offsets[None, :])
    live = live.astype(jnp.int32)

    smem = pl.BlockSpec(memory_space=pltpu.SMEM)
    head_spec = pl.BlockSpec((heads, BLK, size), lambda i: (0, i, 0))
    whole = pl.BlockSpec((rows, size), lambda i: (0, 0))
    far_spec = pl.BlockSpec((len(far), BLK, size), lambda i: (0, i, 0))
    lanes = heads * BLK
    stat_spec = pl.BlockSpec((1, 8, lanes), lambda i: (i, 0, 0))
    acc_spec = pl.BlockSpec((1, size, lanes), lambda i: (i, 0, 0))
    ds_spec = pl.BlockSpec((1, len(far) * BLK, lanes), lambda i: (i, 0, 0))
    stat_shape = jax.ShapeDtypeStruct((blocks, 8, lanes), F32)
    acc_shape = jax.ShapeDtypeStruct((blocks, size, lanes), F32)
    ds_shape = jax.ShapeDtypeStruct((blocks, len(far) * BLK, lanes), BF16)
    far_shape = jax.ShapeDtypeStruct((len(far), rows, size), BF16)
    head_shape = jax.ShapeDtypeStruct(queries.shape, BF16)
    sum_shape = jax.ShapeDtypeStruct((rows, size), F32)

    def cost(slots, matmuls):
        return pl.CostEstimate(
            flops=2 * matmuls * slots * BLK * blocks * lanes * size,
            bytes_accessed=4 * queries.size,
            transcendentals=slots * BLK * blocks * lanes,
        )

    params = pltpu.CompilerParams(dimension_semantics=("arbitrary",), vmem_limit_bytes=40 << 20)
    with jax.named_scope("near_forward"):
        stats, acc = pl.pallas_call(
            functools.partial(near_forward, near, pairs),
            grid=(blocks,),
            in_specs=[smem, head_spec, whole, whole, whole, whole],
            out_specs=[stat_spec, acc_spec],
            out_shape=[stat_shape, acc_shape],
            scratch_shapes=[pltpu.VMEM((2 * rows, size), BF16), pltpu.VMEM((size, 2 * rows), BF16)],
            compiler_params=params,
            cost_estimate=cost(len(near), 2),
            name="near_forward",
        )(live, queries, keys, values, k_prev, v_prev)
    with jax.named_scope("far_both"):
        output, dk_far, dv_far, ds_far, fin = pl.pallas_call(
            functools.partial(far_both, far, pairs),
            grid=(blocks,),
            in_specs=[smem, head_spec, head_spec, far_spec, far_spec, stat_spec, acc_spec],
            out_specs=[head_spec, far_spec, far_spec, ds_spec, stat_spec],
            out_shape=[head_shape, far_shape, far_shape, ds_shape, stat_shape],
            compiler_params=params,
            cost_estimate=cost(len(far), 5),
            name="far_both",
        )(live, queries, out_grad, k_far, v_far, stats, acc)
    with jax.named_scope("near_backward"):
        query_grad, dk_own, dv_own, dk_prev, dv_prev = pl.pallas_call(
            functools.partial(near_backward, near, pairs),
            grid=(blocks,),
            in_specs=[smem, head_spec, head_spec, whole, whole, whole, whole, far_spec, stat_spec, ds_spec],
            out_specs=[head_spec, whole, whole, whole, whole],
            out_shape=[head_shape, sum_shape, sum_shape, sum_shape, sum_shape],
            scratch_shapes=[
                pltpu.VMEM((2 * rows, size), BF16),
                pltpu.VMEM((2 * rows, size), BF16),
                pltpu.VMEM((2 * rows, size), F32),
                pltpu.VMEM((2 * rows, size), F32),
            ],
            compiler_params=params,
            cost_estimate=cost(len(near), 5),
            name="near_backward",
        )(live, queries, out_grad, keys, values, k_prev, v_prev, k_far, fin, ds_far)

    def send_back(pending, prev, own, name):
        arrived = None
        levels = [(hop, pending[n].astype(F32)) for n, hop in enumerate(hops)]
        levels = [(1, prev)] + levels
        for n in reversed(range(len(levels))):
            hop, mine = levels[n]
            below = levels[n - 1][0] if n > 0 else 0
            running = mine if arrived is None else mine + arrived.astype(F32)
            with jax.named_scope(f"back_{name}{hop}"):
                arrived = shift(running.astype(BF16), "ctx", below - hop)
        return (own + arrived.astype(F32)).astype(BF16)[None]

    value_grad = send_back(dv_far, dv_prev, dv_own, "v")
    key_grad = send_back(dk_far, dk_prev, dk_own, "k")
    return output, query_grad, key_grad, value_grad


def solution(mesh):
    split = P(("groups", "head"), "ctx", None)
    return jax.shard_map(
        local,
        mesh=mesh,
        in_specs=(split, split, split, split, P(("groups", "ctx"), None)),
        out_specs=(split, split, split, split),
        check_vma=False,
    )
```

```python
import functools
import math

import jax
import jax.numpy as jnp
from jax import lax
from jax.experimental import pallas as pl
from jax.experimental.pallas import tpu as pltpu
from jax.sharding import PartitionSpec as P


BLK = 128
NOFF = 11
WIDE = 8
FAR_WIDE = 8
BACK_WIDE = 2
NEG = -1e30
LOG2E = 1.4426950408889634
F32 = jnp.float32
BF16 = jnp.bfloat16


def shift(value, axis, steps, holders):
    count = lax.axis_size(axis)
    return lax.ppermute(value, axis, [(n, n + steps) for n in range(holders, count) if 0 <= n + steps < count])


def slot_table(block_count, ctx_size):
    entries = []
    for slot_id in range(NOFF):
        offset = 0 if slot_id == 0 else 2 ** (slot_id - 1)
        if offset < block_count:
            entries.append((slot_id, offset, 0))
        elif offset // block_count < ctx_size:
            entries.append((slot_id, offset, offset // block_count))
    return entries


def dot_nt(a, b):
    return lax.dot_general(a, b, (((1,), (1,)), ((), ())), preferred_element_type=F32)


def dot_nn(a, b):
    return lax.dot_general(a, b, (((1,), (0,)), ((), ())), preferred_element_type=F32)


def block(n):
    return slice(n * BLK, (n + 1) * BLK)


def stack(parts, axis=0):
    return parts[0] if len(parts) == 1 else jnp.concatenate(parts, axis=axis)


class Plan:
    def __init__(self, blocks, heads, size, ctx_size):
        self.blocks, self.heads, self.size = blocks, heads, size
        self.entries = slot_table(blocks, ctx_size)
        self.lanes = heads * BLK
        near = [(n, e[1]) for n, e in enumerate(self.entries) if e[1] <= blocks]
        self.far = [n for n, e in enumerate(self.entries) if e[1] > blocks]
        self.hops = [self.entries[n][2] for n in self.far]
        self.own = [[(n, i - o) for n, o in near if o <= i] for i in range(blocks)]
        self.prev = [[(n, i - o + blocks) for n, o in near if o > i] for i in range(blocks)]
        self.own_at = [sum(len(s) for s in self.own[:i]) for i in range(blocks + 1)]
        self.prev_at = [sum(len(s) for s in self.prev[:i]) for i in range(blocks + 1)]
        self.scale = LOG2E / math.sqrt(size)
        self.inv_root = 1.0 / math.sqrt(size)

    def chunks(self, wide):
        for first in range(0, self.heads, wide):
            yield slice(first, first + wide), slice(first * BLK, (first + wide) * BLK)

    def items(self, wide, rows=None):
        for i in range(self.blocks) if rows is None else rows:
            for heads, lanes in self.chunks(wide):
                yield i, heads, lanes


def rows_of(ref, heads, i, size):
    return ref[heads, block(i)].reshape(-1, size)


def with_ones(values_t):
    width = values_t.shape[1]
    row = lax.broadcasted_iota(jnp.int32, (16, width), 0)
    return jnp.concatenate([values_t, jnp.where(row == 0, 1.0, 0.0).astype(BF16)], axis=0)


def scores_of(plan, raw, biases, mask, top):
    parts = [raw[block(n)] for n in range(len(biases))]
    if mask is not None:
        parts[0] = parts[0] + mask
    for part, bias in zip(parts, biases):
        high = jnp.max(part, axis=0, keepdims=True) * plan.scale
        if bias is not None:
            high = high + bias
        top = high if top is None else jnp.maximum(top, high)
    exps = []
    for part, bias in zip(parts, biases):
        base = top if bias is None else top - bias
        exps.append(jnp.exp2(part * plan.scale - base))
    return exps, top


def staged(items, first, second):
    items = list(items)
    ahead = first(items[0])
    for n, item in enumerate(items):
        now = ahead
        if n + 1 < len(items):
            ahead = first(items[n + 1])
        second(item, now)


def causal_mask(plan, mask_ref):
    key = lax.broadcasted_iota(jnp.int32, mask_ref.shape, 0)
    row = lax.broadcasted_iota(jnp.int32, mask_ref.shape, 1)
    mask_ref[...] = jnp.where(key <= lax.rem(row, BLK), 0.0, NEG)


def local_forward(
    plan, link_ref, causal_ref, q_ref, do_ref, k_ref, v_ref, bias_ref, stat_ref, acc_ref, p_ref, dot_ref
):
    first_block = lax.axis_index("ctx") * plan.blocks
    scalars = []
    for i in range(plan.blocks):
        scalars.append([])
        for n, (slot_id, offset, _) in enumerate(plan.entries):
            live = (link_ref[i, slot_id] == 1) & (first_block + i >= offset)
            scalars[i].append(jnp.where(live, 0.0, NEG).astype(F32))
            bias_ref[i, n : n + 1, :] = jnp.full((1, plan.lanes), scalars[i][n], F32)
    values_t = with_ones(v_ref[0].T)
    size = plan.size

    def first(item):
        i, heads, _ = item
        keys = stack([k_ref[0, block(b)] for _, b in plan.own[i]])
        return dot_nt(keys, rows_of(q_ref, heads, i, size))

    def second(item, raw):
        i, heads, lanes = item
        slots = plan.own[i]
        vt = stack([values_t[:, block(b)] for _, b in slots], axis=1)
        biases = [scalars[i][n] if plan.entries[n][1] > 0 else None for n, _ in slots]
        at = plan.own_at[i] * BLK
        exps, top = scores_of(plan, raw, biases, causal_ref[:, lanes], None)
        low = stack([part.astype(BF16) for part in exps])
        p_ref[at : at + low.shape[0], lanes] = low
        stat_ref[i, 0:1, lanes] = top
        acc_ref[i, :, lanes] = dot_nn(vt, low)[: size + 8]
        dot_ref[i, :, lanes] = rows_of(do_ref, heads, i, size).T

    staged(plan.items(WIDE), first, second)


def prev_forward(plan, q_ref, k_ref, v_ref, dot_ref, bias_ref, stat_in, acc_in, stat_ref, acc_ref, p_ref):
    size = plan.size
    values_t = with_ones(v_ref[...].T)

    def first(item):
        i, heads, _ = item
        keys = stack([k_ref[block(b)] for _, b in plan.prev[i]])
        return dot_nt(keys, rows_of(q_ref, heads, i, size))

    def second(item, raw):
        i, _, lanes = item
        slots = plan.prev[i]
        vt = stack([values_t[:, block(b)] for _, b in slots], axis=1)
        at = plan.prev_at[i] * BLK
        before = stat_in[i, 0:1, lanes]
        biases = [bias_ref[i, n : n + 1, lanes] for n, _ in slots]
        exps, top = scores_of(plan, raw, biases, None, before)
        low = stack([part.astype(BF16) for part in exps])
        p_ref[at : at + low.shape[0], lanes] = low
        acc = acc_in[i, :, lanes] * jnp.exp2(before - top) + dot_nn(vt, low)[: size + 8]
        acc_ref[i, :, lanes] = acc
        stat_ref[i, 0:1, lanes] = before
        stat_ref[i, 1:2, lanes] = top
        stat_ref[i, 2:3, lanes] = jnp.sum(acc[:size] * dot_ref[i, :, lanes].astype(F32), axis=0, keepdims=True)

    staged(plan.items(WIDE), first, second)


def far_scores(plan, q_ref, dot_ref, k_ref, bias_ref, stat_ref, acc_ref, dv_ref, low_ref, fin_ref):
    size = plan.size
    count = len(plan.far)

    def first(item):
        i, heads, _ = item
        keys = stack([k_ref[f, block(i)] for f in range(count)])
        return dot_nt(keys, rows_of(q_ref, heads, i, size))

    def second(item, raw):
        i, _, lanes = item
        before = stat_ref[i, 1:2, lanes]
        biases = [bias_ref[i, n : n + 1, lanes] for n in plan.far]
        exps, top = scores_of(plan, raw, biases, None, before)
        fade = jnp.exp2(before - top)
        total = acc_ref[i, size : size + 1, lanes] * fade
        total = total + sum(jnp.sum(part, axis=0, keepdims=True) for part in exps)
        inverse = 1.0 / total
        low_ref[i, :, lanes] = (stack(exps) * inverse).astype(BF16)
        fin_ref[i, 0:1, lanes] = jnp.exp2(stat_ref[i, 0:1, lanes] - top) * inverse
        fin_ref[i, 1:2, lanes] = fade * inverse
        fin_ref[i, 2:3, lanes] = stat_ref[i, 2:3, lanes] * (fade * inverse)
        if lanes.stop == plan.lanes:
            dv = dot_nt(low_ref[i], dot_ref[i])
            for f in range(count):
                dv_ref[f, block(i)] = dv[block(f)].astype(BF16)

    staged(plan.items(FAR_WIDE), first, second)


def far_keys(plan, q_ref, dot_ref, v_ref, low_ref, fin_in, dk_ref, ds_ref, fin_ref):
    size = plan.size
    count = len(plan.far)

    def first(item):
        i, _, lanes = item
        values = stack([v_ref[f, block(i)] for f in range(count)])
        return dot_nn(values, dot_ref[i, :, lanes])

    def second(item, grad_w):
        i, _, lanes = item
        weights = low_ref[i, :, lanes].astype(F32)
        products = weights * grad_w
        row_dot = fin_in[i, 2:3, lanes] + jnp.sum(products, axis=0, keepdims=True)
        ds_ref[i, :, lanes] = (products - weights * row_dot).astype(BF16)
        fin_ref[i, 0:2, lanes] = fin_in[i, 0:2, lanes]
        fin_ref[i, 2:3, lanes] = row_dot
        if lanes.stop == plan.lanes:
            dk = dot_nn(ds_ref[i], rows_of(q_ref, slice(0, plan.heads), i, size)) * plan.inv_root
            for f in range(count):
                dk_ref[f, block(i)] = dk[block(f)].astype(BF16)

    staged(plan.items(FAR_WIDE), first, second)


def add_blocks(sums, slots, parts):
    for n, (_, b) in enumerate(slots):
        part = parts[block(n)]
        sums[b] = part if b not in sums else sums[b] + part


def scale_rows(plan, i, factor, dot_ref, fin_ref, scaled_ref):
    for heads, lanes in plan.chunks(BACK_WIDE):
        fade = fin_ref[i, factor : factor + 1, lanes]
        scaled_ref[i, :, lanes] = (dot_ref[i, :, lanes].astype(F32) * fade).astype(BF16)


def score_grads(plan, i, slots, values, factor, fin_ref, p_ref, p_at, ds_ref, ds_at, scaled_ref):
    tall = len(slots) * BLK
    for heads, lanes in plan.chunks(BACK_WIDE):
        fade = fin_ref[i, factor : factor + 1, lanes]
        shifted = dot_nn(values, scaled_ref[i, :, lanes]) - fin_ref[i, 2:3, lanes] * fade
        ds_ref[ds_at : ds_at + tall, lanes] = (p_ref[p_at : p_at + tall, lanes].astype(F32) * shifted).astype(BF16)


def prev_values(plan, dot_ref, fin_ref, p_ref, dv_ref, scaled_ref):
    sums = {}
    for i in range(plan.blocks):
        scale_rows(plan, i, 1, dot_ref, fin_ref, scaled_ref)
        part = p_ref[plan.prev_at[i] * BLK : plan.prev_at[i + 1] * BLK, :]
        add_blocks(sums, plan.prev[i], dot_nt(part, scaled_ref[i]))
    for b in range(plan.blocks):
        dv_ref[block(b)] = sums[b]


def prev_keys(plan, q_ref, v_ref, fin_ref, p_ref, scaled_ref, dk_ref, ds_ref):
    sums = {}
    for i in range(plan.blocks):
        slots = plan.prev[i]
        values = stack([v_ref[block(b)] for _, b in slots])
        at, end = plan.prev_at[i] * BLK, plan.prev_at[i + 1] * BLK
        score_grads(plan, i, slots, values, 1, fin_ref, p_ref, at, ds_ref, at, scaled_ref)
        dk = dot_nn(ds_ref[at:end, :], rows_of(q_ref, slice(0, plan.heads), i, plan.size))
        add_blocks(sums, slots, dk)
    for b in range(plan.blocks):
        dk_ref[block(b)] = sums[b] * plan.inv_root


def local_backward(
    plan, q_ref, dot_ref, k_ref, v_ref, kp_ref, kf_ref, vf_ref, fin_ref, acc_ref, low_ref, p_ref, dsp_ref, dsf_ref,
    dk_ref, dv_ref, o_hbm, dq_hbm, scaled_ref, ds_ref, o_ref, dq_ref, sems,
):
    size = plan.size
    count = len(plan.far)
    copies = []

    def send(source, target, i):
        copies.append(pltpu.make_async_copy(source.at[:, block(i)], target.at[:, block(i)], sems.at[len(copies)]))
        copies[-1].start()

    for i in range(plan.blocks):
        vt = stack([vf_ref[f, block(i)] for f in range(count)]).T
        for heads, lanes in plan.chunks(BACK_WIDE):
            out_t = acc_ref[i, :size, lanes] * fin_ref[i, 1:2, lanes] + dot_nn(vt, low_ref[i, :, lanes])
            o_ref[heads, block(i)] = out_t.astype(BF16).T.reshape(BACK_WIDE, BLK, size)
        send(o_ref, o_hbm, i)
    dk_sums, dv_sums = {}, {}
    keys_t = k_ref[...].T
    prev_t = kp_ref[...].T
    for i in range(plan.blocks):
        slots = plan.own[i]
        values = stack([v_ref[block(b)] for _, b in slots])
        at, end = plan.own_at[i] * BLK, plan.own_at[i + 1] * BLK
        scale_rows(plan, i, 0, dot_ref, fin_ref, scaled_ref)
        score_grads(plan, i, slots, values, 0, fin_ref, p_ref, at, ds_ref, at, scaled_ref)
        kt = [keys_t[:, block(b)] for _, b in slots]
        kt += [prev_t[:, block(b)] for _, b in plan.prev[i]]
        kt += [kf_ref[f, block(i)].T for f in range(count)]
        kt = stack(kt, axis=1)
        for heads, lanes in plan.chunks(BACK_WIDE):
            ds = [ds_ref[at:end, lanes]]
            if plan.prev[i]:
                ds.append(dsp_ref[plan.prev_at[i] * BLK : plan.prev_at[i + 1] * BLK, lanes])
            if count:
                ds.append(dsf_ref[i, :, lanes])
            dq_t = (dot_nn(kt, stack(ds)) * plan.inv_root).astype(BF16)
            dq_ref[heads, block(i)] = dq_t.T.reshape(BACK_WIDE, BLK, size)
        send(dq_ref, dq_hbm, i)
        add_blocks(dv_sums, slots, dot_nt(p_ref[at:end, :], scaled_ref[i]))
        add_blocks(dk_sums, slots, dot_nn(ds_ref[at:end, :], rows_of(q_ref, slice(0, plan.heads), i, size)))
    for b in range(plan.blocks):
        dk_ref[block(b)] = dk_sums[b] * plan.inv_root
        dv_ref[block(b)] = dv_sums[b]
    for copy in copies:
        copy.wait()


def local(queries, key_rows, value_rows, out_grad, link_mask):
    heads, rows, size = queries.shape
    blocks = rows // BLK
    plan = Plan(blocks, heads, size, lax.axis_size("ctx"))
    lanes = plan.lanes
    count = len(plan.far)

    keys, values = key_rows[0], value_rows[0]
    k_prev = shift(keys, "ctx", 1, 0)
    v_prev = shift(values, "ctx", 1, 0)
    k_far, v_far = [], []
    k_last, v_last, at = k_prev, v_prev, 1
    for hop in plan.hops:
        k_last = shift(k_last, "ctx", hop - at, at)
        v_last = shift(v_last, "ctx", hop - at, at)
        at = hop
        k_far.append(k_last)
        v_far.append(v_last)
    if count == 1:
        k_far, v_far = k_far[0][None], v_far[0][None]
    else:
        k_far, v_far = jnp.stack(k_far), jnp.stack(v_far)

    def array(*shape, dtype=BF16):
        return jax.ShapeDtypeStruct(shape, dtype)

    vmem = pl.BlockSpec(memory_space=pltpu.VMEM)
    smem = pl.BlockSpec(memory_space=pltpu.SMEM)
    hbm = pl.BlockSpec(memory_space=pltpu.HBM)

    def call(body, slots, matmuls, outs, operands, scratch=(), places=None, lasts=(), alias=None):
        flops = 2 * matmuls * slots * BLK * lanes * size
        return pl.pallas_call(
            functools.partial(body, plan),
            in_specs=places or [vmem] * len(operands),
            out_specs=[vmem] * (len(outs) - len(lasts)) + list(lasts),
            out_shape=outs,
            scratch_shapes=list(scratch),
            input_output_aliases=alias or {},
            compiler_params=pltpu.CompilerParams(vmem_limit_bytes=20 << 20),
            cost_estimate=pl.CostEstimate(
                flops=flops, bytes_accessed=4 * queries.size, transcendentals=slots * BLK * lanes
            ),
        )(*operands)

    n_own, n_prev, n_far = plan.own_at[-1], plan.prev_at[-1], count * blocks
    stat = array(blocks, 8, lanes, dtype=F32)
    acc = array(blocks, size + 8, lanes, dtype=F32)
    total = array(rows, size, dtype=F32)
    bias = array(blocks, 16, lanes, dtype=F32)
    grads_t = array(blocks, size, lanes)
    own_shape, prev_shape = array(n_own * BLK, lanes), array(n_prev * BLK, lanes)
    ds_shape = array(blocks, count * BLK, lanes)
    far_shape = array(count, rows, size)
    full = array(*queries.shape)
    whole = pltpu.VMEM(queries.shape, BF16)

    causal = call(causal_mask, n_own, 8, [array(BLK, lanes, dtype=F32)], ())[0]
    bias, stat_own, acc_own, p_own, grad_t = call(
        local_forward, n_own, 2,
        [bias, stat, acc, own_shape, grads_t],
        (link_mask, causal, queries, out_grad, key_rows, value_rows),
        places=[smem] + [vmem] * 5,
    )
    stat_near, acc_near, p_prev = call(
        prev_forward, n_prev, 2,
        [stat, acc, prev_shape],
        (queries, k_prev, v_prev, grad_t, bias, stat_own, acc_own),
    )
    dv_far, low_far, fin = call(
        far_scores, n_far, 2,
        [far_shape, ds_shape, stat],
        (queries, grad_t, k_far, bias, stat_near, acc_near),
    )
    dk_far, ds_far, fin = call(
        far_keys, n_far, 2,
        [far_shape, ds_shape, stat],
        (queries, grad_t, v_far, low_far, fin),
    )
    dv_prev, scaled = call(prev_values, n_prev, 1, [total, grads_t], (grad_t, fin, p_prev))
    dk_prev, ds_prev = call(prev_keys, n_prev, 2, [total, prev_shape], (queries, v_prev, fin, p_prev, scaled))
    dk_own, dv_own, output, query_grad = call(
        local_backward, n_own, 5,
        [total, total, full, full],
        (queries, grad_t, keys, values, k_prev, k_far, v_far, fin, acc_near, low_far, p_own, ds_prev, ds_far),
        scratch=[
            pltpu.VMEM(grads_t.shape, BF16), pltpu.VMEM(own_shape.shape, BF16), whole, whole, pltpu.SemaphoreType.DMA((2 * blocks,))
        ],
        lasts=(hbm, hbm),
    )

    def send_back(pending, prev, own):
        levels = [(1, prev)] + [(hop, pending[n].astype(F32)) for n, hop in enumerate(plan.hops)]
        arrived = None
        for n in reversed(range(len(levels))):
            hop, mine = levels[n]
            below = levels[n - 1][0] if n > 0 else 0
            running = mine if arrived is None else mine + arrived.astype(F32)
            arrived = shift(running.astype(BF16), "ctx", below - hop, hop)
        return (own + arrived.astype(F32)).astype(BF16)[None]

    value_grad = send_back(dv_far, dv_prev, dv_own)
    key_grad = send_back(dk_far, dk_prev, dk_own)
    return output, query_grad, key_grad, value_grad


def solution(mesh):
    split = P(("groups", "head"), "ctx", None)

    return jax.shard_map(
        local,
        mesh=mesh,
        in_specs=(split, split, split, split, P(("groups", "ctx"), None)),
        out_specs=(split, split, split, split),
        check_vma=False,
    )
```

```python
import functools
import math

import jax
import jax.numpy as jnp
from jax import lax
from jax.experimental import pallas as pl
from jax.experimental.pallas import tpu as pltpu
from jax.sharding import PartitionSpec as P


BLK = 128
NOFF = 11
WIDE = 8
FAR_WIDE = 8
BACK_WIDE = 2
NEG = -1e30
LOG2E = 1.4426950408889634
F32 = jnp.float32
BF16 = jnp.bfloat16


def shift(value, axis, steps, holders):
    count = lax.axis_size(axis)
    return lax.ppermute(value, axis, [(n, n + steps) for n in range(holders, count) if 0 <= n + steps < count])


def slot_table(block_count, ctx_size):
    entries = []
    for slot_id in range(NOFF):
        offset = 0 if slot_id == 0 else 2 ** (slot_id - 1)
        if offset < block_count:
            entries.append((slot_id, offset, 0))
        elif offset // block_count < ctx_size:
            entries.append((slot_id, offset, offset // block_count))
    return entries


def dot_nt(a, b):
    return lax.dot_general(a, b, (((1,), (1,)), ((), ())), preferred_element_type=F32)


def dot_nn(a, b):
    return lax.dot_general(a, b, (((1,), (0,)), ((), ())), preferred_element_type=F32)


def block(n):
    return slice(n * BLK, (n + 1) * BLK)


def stack(parts, axis=0):
    return parts[0] if len(parts) == 1 else jnp.concatenate(parts, axis=axis)


class Plan:
    def __init__(self, blocks, heads, size, ctx_size):
        self.blocks, self.heads, self.size = blocks, heads, size
        self.entries = slot_table(blocks, ctx_size)
        self.lanes = heads * BLK
        near = [(n, e[1]) for n, e in enumerate(self.entries) if e[1] <= blocks]
        self.far = [n for n, e in enumerate(self.entries) if e[1] > blocks]
        self.hops = [self.entries[n][2] for n in self.far]
        self.own = [[(n, i - o) for n, o in near if o <= i] for i in range(blocks)]
        self.prev = [[(n, i - o + blocks) for n, o in near if o > i] for i in range(blocks)]
        self.own_at = [sum(len(s) for s in self.own[:i]) for i in range(blocks + 1)]
        self.prev_at = [sum(len(s) for s in self.prev[:i]) for i in range(blocks + 1)]
        self.scale = LOG2E / math.sqrt(size)
        self.inv_root = 1.0 / math.sqrt(size)

    def chunks(self, wide):
        for first in range(0, self.heads, wide):
            yield slice(first, first + wide), slice(first * BLK, (first + wide) * BLK)

    def items(self, wide, rows=None):
        for i in range(self.blocks) if rows is None else rows:
            for heads, lanes in self.chunks(wide):
                yield i, heads, lanes


def rows_of(ref, heads, i, size):
    return ref[heads, block(i)].reshape(-1, size)


def with_ones(values_t):
    width = values_t.shape[1]
    row = lax.broadcasted_iota(jnp.int32, (16, width), 0)
    return jnp.concatenate([values_t, jnp.where(row == 0, 1.0, 0.0).astype(BF16)], axis=0)


def scores_of(plan, raw, biases, mask, top):
    parts = [raw[block(n)] for n in range(len(biases))]
    if mask is not None:
        parts[0] = parts[0] + mask
    for part, bias in zip(parts, biases):
        high = jnp.max(part, axis=0, keepdims=True) * plan.scale
        if bias is not None:
            high = high + bias
        top = high if top is None else jnp.maximum(top, high)
    exps = []
    for part, bias in zip(parts, biases):
        base = top if bias is None else top - bias
        exps.append(jnp.exp2(part * plan.scale - base))
    return exps, top


def staged(items, first, second):
    items = list(items)
    ahead = first(items[0])
    for n, item in enumerate(items):
        now = ahead
        if n + 1 < len(items):
            ahead = first(items[n + 1])
        second(item, now)


def causal_mask(plan, mask_ref):
    key = lax.broadcasted_iota(jnp.int32, mask_ref.shape, 0)
    row = lax.broadcasted_iota(jnp.int32, mask_ref.shape, 1)
    mask_ref[...] = jnp.where(key <= lax.rem(row, BLK), 0.0, NEG)


def local_forward(
    plan, link_ref, causal_ref, q_ref, do_ref, k_ref, v_ref, bias_ref, stat_ref, acc_ref, p_ref, dot_ref
):
    first_block = lax.axis_index("ctx") * plan.blocks
    scalars = []
    for i in range(plan.blocks):
        scalars.append([])
        for n, (slot_id, offset, _) in enumerate(plan.entries):
            live = (link_ref[i, slot_id] == 1) & (first_block + i >= offset)
            scalars[i].append(jnp.where(live, 0.0, NEG).astype(F32))
            bias_ref[i, n : n + 1, :] = jnp.full((1, plan.lanes), scalars[i][n], F32)
    values_t = with_ones(v_ref[0].T)
    size = plan.size

    def first(item):
        i, heads, _ = item
        keys = stack([k_ref[0, block(b)] for _, b in plan.own[i]])
        return dot_nt(keys, rows_of(q_ref, heads, i, size))

    def second(item, raw):
        i, heads, lanes = item
        slots = plan.own[i]
        vt = stack([values_t[:, block(b)] for _, b in slots], axis=1)
        biases = [scalars[i][n] if plan.entries[n][1] > 0 else None for n, _ in slots]
        at = plan.own_at[i] * BLK
        exps, top = scores_of(plan, raw, biases, causal_ref[:, lanes], None)
        low = stack([part.astype(BF16) for part in exps])
        p_ref[at : at + low.shape[0], lanes] = low
        stat_ref[i, 0:1, lanes] = top
        acc_ref[i, :, lanes] = dot_nn(vt, low)[: size + 8]
        dot_ref[i, :, lanes] = rows_of(do_ref, heads, i, size).T

    staged(plan.items(WIDE), first, second)


def prev_forward(plan, q_ref, k_ref, v_ref, dot_ref, bias_ref, stat_in, acc_in, stat_ref, acc_ref, p_ref):
    size = plan.size
    values_t = with_ones(v_ref[...].T)

    def first(item):
        i, heads, _ = item
        keys = stack([k_ref[block(b)] for _, b in plan.prev[i]])
        return dot_nt(keys, rows_of(q_ref, heads, i, size))

    def second(item, raw):
        i, _, lanes = item
        slots = plan.prev[i]
        vt = stack([values_t[:, block(b)] for _, b in slots], axis=1)
        at = plan.prev_at[i] * BLK
        before = stat_in[i, 0:1, lanes]
        biases = [bias_ref[i, n : n + 1, lanes] for n, _ in slots]
        exps, top = scores_of(plan, raw, biases, None, before)
        low = stack([part.astype(BF16) for part in exps])
        p_ref[at : at + low.shape[0], lanes] = low
        acc = acc_in[i, :, lanes] * jnp.exp2(before - top) + dot_nn(vt, low)[: size + 8]
        acc_ref[i, :, lanes] = acc
        stat_ref[i, 0:1, lanes] = before
        stat_ref[i, 1:2, lanes] = top
        stat_ref[i, 2:3, lanes] = jnp.sum(acc[:size] * dot_ref[i, :, lanes].astype(F32), axis=0, keepdims=True)

    staged(plan.items(WIDE), first, second)


def has_far(plan):
    return (lax.axis_index("ctx") + 1) * plan.blocks > plan.entries[plan.far[0]][1]


def far_scores(plan, q_ref, dot_ref, k_ref, bias_ref, stat_ref, acc_ref, dv_ref, low_ref, fin_ref):
    size = plan.size
    count = len(plan.far)

    def first(item):
        i, heads, _ = item
        keys = stack([k_ref[f, block(i)] for f in range(count)])
        return dot_nt(keys, rows_of(q_ref, heads, i, size))

    def second(item, raw):
        i, _, lanes = item
        before = stat_ref[i, 1:2, lanes]
        biases = [bias_ref[i, n : n + 1, lanes] for n in plan.far]
        exps, top = scores_of(plan, raw, biases, None, before)
        fade = jnp.exp2(before - top)
        total = acc_ref[i, size : size + 1, lanes] * fade
        total = total + sum(jnp.sum(part, axis=0, keepdims=True) for part in exps)
        inverse = 1.0 / total
        low_ref[i, :, lanes] = (stack(exps) * inverse).astype(BF16)
        fin_ref[i, 0:1, lanes] = jnp.exp2(stat_ref[i, 0:1, lanes] - top) * inverse
        fin_ref[i, 1:2, lanes] = fade * inverse
        fin_ref[i, 2:3, lanes] = stat_ref[i, 2:3, lanes] * (fade * inverse)
        if lanes.stop == plan.lanes:
            dv = dot_nt(low_ref[i], dot_ref[i])
            for f in range(count):
                dv_ref[f, block(i)] = dv[block(f)].astype(BF16)

    @pl.when(has_far(plan))
    def _():
        staged(plan.items(FAR_WIDE), first, second)

    @pl.when(jnp.logical_not(has_far(plan)))
    def _():
        dv_ref[...] = jnp.zeros_like(dv_ref)
        low_ref[...] = jnp.zeros_like(low_ref)
        for i in range(plan.blocks):
            inverse = 1.0 / acc_ref[i, size : size + 1, :]
            fin_ref[i, 0:1, :] = jnp.exp2(stat_ref[i, 0:1, :] - stat_ref[i, 1:2, :]) * inverse
            fin_ref[i, 1:2, :] = inverse
            fin_ref[i, 2:3, :] = stat_ref[i, 2:3, :] * inverse


def far_keys(plan, q_ref, dot_ref, v_ref, low_ref, fin_in, dk_ref, ds_ref, fin_ref):
    size = plan.size
    count = len(plan.far)

    def first(item):
        i, _, lanes = item
        values = stack([v_ref[f, block(i)] for f in range(count)])
        return dot_nn(values, dot_ref[i, :, lanes])

    def second(item, grad_w):
        i, _, lanes = item
        weights = low_ref[i, :, lanes].astype(F32)
        products = weights * grad_w
        row_dot = fin_in[i, 2:3, lanes] + jnp.sum(products, axis=0, keepdims=True)
        ds_ref[i, :, lanes] = (products - weights * row_dot).astype(BF16)
        fin_ref[i, 2:3, lanes] = row_dot
        if lanes.stop == plan.lanes:
            dk = dot_nn(ds_ref[i], rows_of(q_ref, slice(0, plan.heads), i, size)) * plan.inv_root
            for f in range(count):
                dk_ref[f, block(i)] = dk[block(f)].astype(BF16)

    fin_ref[...] = fin_in[...]

    @pl.when(has_far(plan))
    def _():
        staged(plan.items(FAR_WIDE), first, second)

    @pl.when(jnp.logical_not(has_far(plan)))
    def _():
        dk_ref[...] = jnp.zeros_like(dk_ref)
        ds_ref[...] = jnp.zeros_like(ds_ref)


def add_blocks(sums, slots, parts):
    for n, (_, b) in enumerate(slots):
        part = parts[block(n)]
        sums[b] = part if b not in sums else sums[b] + part


def scale_rows(plan, i, factor, dot_ref, fin_ref, scaled_ref):
    for heads, lanes in plan.chunks(BACK_WIDE):
        fade = fin_ref[i, factor : factor + 1, lanes]
        scaled_ref[i, :, lanes] = (dot_ref[i, :, lanes].astype(F32) * fade).astype(BF16)


def score_grads(plan, i, slots, values, factor, fin_ref, p_ref, p_at, ds_ref, ds_at, scaled_ref):
    tall = len(slots) * BLK
    for heads, lanes in plan.chunks(BACK_WIDE):
        fade = fin_ref[i, factor : factor + 1, lanes]
        shifted = dot_nn(values, scaled_ref[i, :, lanes]) - fin_ref[i, 2:3, lanes] * fade
        ds_ref[ds_at : ds_at + tall, lanes] = (p_ref[p_at : p_at + tall, lanes].astype(F32) * shifted).astype(BF16)


def prev_values(plan, dot_ref, fin_ref, p_ref, dv_ref, scaled_ref):
    sums = {}
    for i in range(plan.blocks):
        scale_rows(plan, i, 1, dot_ref, fin_ref, scaled_ref)
        part = p_ref[plan.prev_at[i] * BLK : plan.prev_at[i + 1] * BLK, :]
        add_blocks(sums, plan.prev[i], dot_nt(part, scaled_ref[i]))
    for b in range(plan.blocks):
        dv_ref[block(b)] = sums[b]


def prev_keys(plan, q_ref, v_ref, fin_ref, p_ref, scaled_ref, dk_ref, ds_ref):
    sums = {}
    for i in range(plan.blocks):
        slots = plan.prev[i]
        values = stack([v_ref[block(b)] for _, b in slots])
        at, end = plan.prev_at[i] * BLK, plan.prev_at[i + 1] * BLK
        score_grads(plan, i, slots, values, 1, fin_ref, p_ref, at, ds_ref, at, scaled_ref)
        dk = dot_nn(ds_ref[at:end, :], rows_of(q_ref, slice(0, plan.heads), i, plan.size))
        add_blocks(sums, slots, dk)
    for b in range(plan.blocks):
        dk_ref[block(b)] = sums[b] * plan.inv_root


def local_backward(
    plan, q_ref, dot_ref, k_ref, v_ref, kp_ref, kf_ref, vf_ref, fin_ref, acc_ref, low_ref, p_ref, dsp_ref, dsf_ref,
    dk_ref, dv_ref, o_hbm, dq_hbm, scaled_ref, ds_ref, o_ref, dq_ref, sems,
):
    size = plan.size
    count = len(plan.far)
    copies = []

    def send(source, target, i):
        copies.append(pltpu.make_async_copy(source.at[:, block(i)], target.at[:, block(i)], sems.at[len(copies)]))
        copies[-1].start()

    for i in range(plan.blocks):
        vt = stack([vf_ref[f, block(i)] for f in range(count)]).T
        for heads, lanes in plan.chunks(BACK_WIDE):
            out_t = acc_ref[i, :size, lanes] * fin_ref[i, 1:2, lanes] + dot_nn(vt, low_ref[i, :, lanes])
            o_ref[heads, block(i)] = out_t.astype(BF16).T.reshape(BACK_WIDE, BLK, size)
        send(o_ref, o_hbm, i)
    dk_sums, dv_sums = {}, {}
    keys_t = k_ref[...].T
    prev_t = kp_ref[...].T
    for i in range(plan.blocks):
        slots = plan.own[i]
        values = stack([v_ref[block(b)] for _, b in slots])
        at, end = plan.own_at[i] * BLK, plan.own_at[i + 1] * BLK
        scale_rows(plan, i, 0, dot_ref, fin_ref, scaled_ref)
        score_grads(plan, i, slots, values, 0, fin_ref, p_ref, at, ds_ref, at, scaled_ref)
        kt = [keys_t[:, block(b)] for _, b in slots]
        kt += [prev_t[:, block(b)] for _, b in plan.prev[i]]
        kt += [kf_ref[f, block(i)].T for f in range(count)]
        kt = stack(kt, axis=1)
        for heads, lanes in plan.chunks(BACK_WIDE):
            ds = [ds_ref[at:end, lanes]]
            if plan.prev[i]:
                ds.append(dsp_ref[plan.prev_at[i] * BLK : plan.prev_at[i + 1] * BLK, lanes])
            if count:
                ds.append(dsf_ref[i, :, lanes])
            dq_t = (dot_nn(kt, stack(ds)) * plan.inv_root).astype(BF16)
            dq_ref[heads, block(i)] = dq_t.T.reshape(BACK_WIDE, BLK, size)
        send(dq_ref, dq_hbm, i)
        add_blocks(dv_sums, slots, dot_nt(p_ref[at:end, :], scaled_ref[i]))
        add_blocks(dk_sums, slots, dot_nn(ds_ref[at:end, :], rows_of(q_ref, slice(0, plan.heads), i, size)))
    for b in range(plan.blocks):
        dk_ref[block(b)] = dk_sums[b] * plan.inv_root
        dv_ref[block(b)] = dv_sums[b]
    for copy in copies:
        copy.wait()


def finish(plan, dk_ref, dv_ref, kg_ref, vg_ref, k_hbm, v_hbm, k_out, v_out, sems):
    copies = []
    for n, (own, arrived, out, target) in enumerate(
        ((dv_ref, vg_ref, v_out, v_hbm), (dk_ref, kg_ref, k_out, k_hbm))
    ):
        out[0] = (own[...] + arrived[...].astype(F32)).astype(BF16)
        copies.append(pltpu.make_async_copy(out, target, sems.at[n]))
        copies[n].start()
    for copy in copies:
        copy.wait()


def local(queries, key_rows, value_rows, out_grad, link_mask):
    heads, rows, size = queries.shape
    blocks = rows // BLK
    plan = Plan(blocks, heads, size, lax.axis_size("ctx"))
    lanes = plan.lanes
    count = len(plan.far)

    keys, values = key_rows[0], value_rows[0]
    k_prev = shift(keys, "ctx", 1, 0)
    v_prev = shift(values, "ctx", 1, 0)
    k_far, v_far = [], []
    k_last, v_last, at = k_prev, v_prev, 1
    for hop in plan.hops:
        k_last = shift(k_last, "ctx", hop - at, at)
        v_last = shift(v_last, "ctx", hop - at, at)
        at = hop
        k_far.append(k_last)
        v_far.append(v_last)
    if count == 1:
        k_far, v_far = k_far[0][None], v_far[0][None]
    else:
        k_far, v_far = jnp.stack(k_far), jnp.stack(v_far)

    def array(*shape, dtype=BF16):
        return jax.ShapeDtypeStruct(shape, dtype)

    vmem = pl.BlockSpec(memory_space=pltpu.VMEM)
    smem = pl.BlockSpec(memory_space=pltpu.SMEM)
    hbm = pl.BlockSpec(memory_space=pltpu.HBM)

    def call(body, slots, matmuls, outs, operands, scratch=(), places=None, lasts=(), alias=None):
        flops = 2 * matmuls * slots * BLK * lanes * size
        return pl.pallas_call(
            functools.partial(body, plan),
            in_specs=places or [vmem] * len(operands),
            out_specs=[vmem] * (len(outs) - len(lasts)) + list(lasts),
            out_shape=outs,
            scratch_shapes=list(scratch),
            input_output_aliases=alias or {},
            compiler_params=pltpu.CompilerParams(vmem_limit_bytes=20 << 20),
            cost_estimate=pl.CostEstimate(
                flops=flops, bytes_accessed=4 * queries.size, transcendentals=slots * BLK * lanes
            ),
        )(*operands)

    n_own, n_prev, n_far = plan.own_at[-1], plan.prev_at[-1], count * blocks
    stat = array(blocks, 8, lanes, dtype=F32)
    acc = array(blocks, size + 8, lanes, dtype=F32)
    total = array(rows, size, dtype=F32)
    bias = array(blocks, 16, lanes, dtype=F32)
    grads_t = array(blocks, size, lanes)
    own_shape, prev_shape = array(n_own * BLK, lanes), array(n_prev * BLK, lanes)
    ds_shape = array(blocks, count * BLK, lanes)
    far_shape = array(count, rows, size)
    full = array(*queries.shape)
    whole = pltpu.VMEM(queries.shape, BF16)

    causal = call(causal_mask, n_own, 8, [array(BLK, lanes, dtype=F32)], ())[0]
    bias, stat_own, acc_own, p_own, grad_t = call(
        local_forward, n_own, 2,
        [bias, stat, acc, own_shape, grads_t],
        (link_mask, causal, queries, out_grad, key_rows, value_rows),
        places=[smem] + [vmem] * 5,
    )
    stat_near, acc_near, p_prev = call(
        prev_forward, n_prev, 2,
        [stat, acc, prev_shape],
        (queries, k_prev, v_prev, grad_t, bias, stat_own, acc_own),
    )
    dv_far, low_far, fin = call(
        far_scores, n_far, 2,
        [far_shape, ds_shape, stat],
        (queries, grad_t, k_far, bias, stat_near, acc_near),
    )
    dk_far, ds_far, fin = call(
        far_keys, n_far, 2,
        [far_shape, ds_shape, stat],
        (queries, grad_t, v_far, low_far, fin),
    )
    dv_prev, scaled = call(prev_values, n_prev, 1, [total, grads_t], (grad_t, fin, p_prev))
    dk_prev, ds_prev = call(prev_keys, n_prev, 2, [total, prev_shape], (queries, v_prev, fin, p_prev, scaled))
    dk_own, dv_own, output, query_grad = call(
        local_backward, n_own, 5,
        [total, total, full, full],
        (queries, grad_t, keys, values, k_prev, k_far, v_far, fin, acc_near, low_far, p_own, ds_prev, ds_far),
        scratch=[
            pltpu.VMEM(grads_t.shape, BF16), pltpu.VMEM(own_shape.shape, BF16), whole, whole, pltpu.SemaphoreType.DMA((2 * blocks,))
        ],
        lasts=(hbm, hbm),
    )

    def send_back(pending, prev):
        levels = [(1, prev)] + [(hop, pending[n].astype(F32)) for n, hop in enumerate(plan.hops)]
        arrived = None
        for n in reversed(range(len(levels))):
            hop, mine = levels[n]
            below = levels[n - 1][0] if n > 0 else 0
            running = mine if arrived is None else mine + arrived.astype(F32)
            arrived = shift(running.astype(BF16), "ctx", below - hop, hop)
        return arrived

    v_arrived = send_back(dv_far, dv_prev)
    k_arrived = send_back(dk_far, dk_prev)
    line = array(1, rows, size)
    key_grad, value_grad = call(
        finish, 1, 1, [line, line], (dk_own, dv_own, k_arrived, v_arrived),
        scratch=[pltpu.VMEM(line.shape, BF16), pltpu.VMEM(line.shape, BF16), pltpu.SemaphoreType.DMA((2,))],
        lasts=(hbm, hbm),
    )
    return output, query_grad, key_grad, value_grad


def solution(mesh):
    split = P(("groups", "head"), "ctx", None)

    return jax.shard_map(
        local,
        mesh=mesh,
        in_specs=(split, split, split, split, P(("groups", "ctx"), None)),
        out_specs=(split, split, split, split),
        check_vma=False,
    )
```

```python
import functools
import math

import jax
import jax.numpy as jnp
from jax import lax
from jax.experimental import pallas as pl
from jax.experimental.pallas import tpu as pltpu
from jax.sharding import PartitionSpec as P


BLK = 128
NOFF = 11
WIDE = 8
FAR_WIDE = 8
BACK_WIDE = 2
NEG = -1e30
LOG2E = 1.4426950408889634
F32 = jnp.float32
BF16 = jnp.bfloat16


def shift(value, axis, steps, holders):
    count = lax.axis_size(axis)
    return lax.ppermute(value, axis, [(n, n + steps) for n in range(holders, count) if 0 <= n + steps < count])


def two_up(own, near, axis):
    count = lax.axis_size(axis)
    straight = lax.ppermute(own, axis, [(n, n + 2) for n in range(0, count - 2, 2)])
    relayed = lax.ppermute(near, axis, [(n, n + 1) for n in range(2, count - 1, 2)])
    return straight + relayed


def far_rows(own, near, hops):
    rows = [two_up(own, near, "ctx")]
    for at, hop in zip(hops, hops[1:]):
        rows.append(shift(rows[-1], "ctx", hop - at, at))
    return rows[0][None] if len(rows) == 1 else jnp.stack(rows)


def slot_table(block_count, ctx_size):
    entries = []
    for slot_id in range(NOFF):
        offset = 0 if slot_id == 0 else 2 ** (slot_id - 1)
        if offset < block_count:
            entries.append((slot_id, offset, 0))
        elif offset // block_count < ctx_size:
            entries.append((slot_id, offset, offset // block_count))
    return entries


def dot_nt(a, b):
    return lax.dot_general(a, b, (((1,), (1,)), ((), ())), preferred_element_type=F32)


def dot_nn(a, b):
    return lax.dot_general(a, b, (((1,), (0,)), ((), ())), preferred_element_type=F32)


def block(n):
    return slice(n * BLK, (n + 1) * BLK)


def stack(parts, axis=0):
    return parts[0] if len(parts) == 1 else jnp.concatenate(parts, axis=axis)


class Plan:
    def __init__(self, blocks, heads, size, ctx_size):
        self.blocks, self.heads, self.size = blocks, heads, size
        self.entries = slot_table(blocks, ctx_size)
        self.lanes = heads * BLK
        near = [(n, e[1]) for n, e in enumerate(self.entries) if e[1] <= blocks]
        self.far = [n for n, e in enumerate(self.entries) if e[1] > blocks]
        self.hops = [self.entries[n][2] for n in self.far]
        self.own = [[(n, i - o) for n, o in near if o <= i] for i in range(blocks)]
        self.prev = [[(n, i - o + blocks) for n, o in near if o > i] for i in range(blocks)]
        self.own_at = [sum(len(s) for s in self.own[:i]) for i in range(blocks + 1)]
        self.prev_at = [sum(len(s) for s in self.prev[:i]) for i in range(blocks + 1)]
        self.scale = LOG2E / math.sqrt(size)
        self.inv_root = 1.0 / math.sqrt(size)

    def chunks(self, wide):
        for first in range(0, self.heads, wide):
            yield slice(first, first + wide), slice(first * BLK, (first + wide) * BLK)

    def items(self, wide, rows=None):
        for i in range(self.blocks) if rows is None else rows:
            for heads, lanes in self.chunks(wide):
                yield i, heads, lanes


def rows_of(ref, heads, i, size):
    return ref[heads, block(i)].reshape(-1, size)


def with_ones(values_t):
    width = values_t.shape[1]
    row = lax.broadcasted_iota(jnp.int32, (16, width), 0)
    return jnp.concatenate([values_t, jnp.where(row == 0, 1.0, 0.0).astype(BF16)], axis=0)


def scores_of(plan, raw, biases, mask, top):
    parts = [raw[block(n)] for n in range(len(biases))]
    if mask is not None:
        parts[0] = parts[0] + mask
    for part, bias in zip(parts, biases):
        high = jnp.max(part, axis=0, keepdims=True) * plan.scale
        if bias is not None:
            high = high + bias
        top = high if top is None else jnp.maximum(top, high)
    exps = []
    for part, bias in zip(parts, biases):
        base = top if bias is None else top - bias
        exps.append(jnp.exp2(part * plan.scale - base))
    return exps, top


def staged(items, first, second):
    items = list(items)
    ahead = first(items[0])
    for n, item in enumerate(items):
        now = ahead
        if n + 1 < len(items):
            ahead = first(items[n + 1])
        second(item, now)


def causal_mask(plan, mask_ref):
    key = lax.broadcasted_iota(jnp.int32, mask_ref.shape, 0)
    row = lax.broadcasted_iota(jnp.int32, mask_ref.shape, 1)
    mask_ref[...] = jnp.where(key <= lax.rem(row, BLK), 0.0, NEG)


def local_forward(
    plan, link_ref, causal_ref, q_ref, do_ref, k_ref, v_ref, bias_ref, stat_ref, acc_ref, p_ref, dot_ref
):
    first_block = lax.axis_index("ctx") * plan.blocks
    scalars = []
    for i in range(plan.blocks):
        scalars.append([])
        for n, (slot_id, offset, _) in enumerate(plan.entries):
            live = (link_ref[i, slot_id] == 1) & (first_block + i >= offset)
            scalars[i].append(jnp.where(live, 0.0, NEG).astype(F32))
            bias_ref[i, n : n + 1, :] = jnp.full((1, plan.lanes), scalars[i][n], F32)
    values_t = with_ones(v_ref[0].T)
    size = plan.size

    def first(item):
        i, heads, _ = item
        keys = stack([k_ref[0, block(b)] for _, b in plan.own[i]])
        return dot_nt(keys, rows_of(q_ref, heads, i, size))

    def second(item, raw):
        i, heads, lanes = item
        slots = plan.own[i]
        vt = stack([values_t[:, block(b)] for _, b in slots], axis=1)
        biases = [scalars[i][n] if plan.entries[n][1] > 0 else None for n, _ in slots]
        at = plan.own_at[i] * BLK
        exps, top = scores_of(plan, raw, biases, causal_ref[:, lanes], None)
        low = stack([part.astype(BF16) for part in exps])
        p_ref[at : at + low.shape[0], lanes] = low
        stat_ref[i, 0:1, lanes] = top
        acc_ref[i, :, lanes] = dot_nn(vt, low)[: size + 8]
        dot_ref[i, :, lanes] = rows_of(do_ref, heads, i, size).T

    staged(plan.items(WIDE), first, second)


def prev_forward(plan, q_ref, k_ref, v_ref, dot_ref, bias_ref, stat_in, acc_in, stat_ref, acc_ref, p_ref):
    size = plan.size
    values_t = with_ones(v_ref[...].T)

    def first(item):
        i, heads, _ = item
        keys = stack([k_ref[block(b)] for _, b in plan.prev[i]])
        return dot_nt(keys, rows_of(q_ref, heads, i, size))

    def second(item, raw):
        i, _, lanes = item
        slots = plan.prev[i]
        vt = stack([values_t[:, block(b)] for _, b in slots], axis=1)
        at = plan.prev_at[i] * BLK
        before = stat_in[i, 0:1, lanes]
        biases = [bias_ref[i, n : n + 1, lanes] for n, _ in slots]
        exps, top = scores_of(plan, raw, biases, None, before)
        low = stack([part.astype(BF16) for part in exps])
        p_ref[at : at + low.shape[0], lanes] = low
        acc = acc_in[i, :, lanes] * jnp.exp2(before - top) + dot_nn(vt, low)[: size + 8]
        acc_ref[i, :, lanes] = acc
        stat_ref[i, 0:1, lanes] = before
        stat_ref[i, 1:2, lanes] = top
        stat_ref[i, 2:3, lanes] = jnp.sum(acc[:size] * dot_ref[i, :, lanes].astype(F32), axis=0, keepdims=True)

    staged(plan.items(WIDE), first, second)


def has_far(plan):
    return (lax.axis_index("ctx") + 1) * plan.blocks > plan.entries[plan.far[0]][1]


def far_scores(plan, q_ref, dot_ref, k_ref, bias_ref, stat_ref, acc_ref, dv_ref, low_ref, fin_ref):
    size = plan.size
    count = len(plan.far)

    def first(item):
        i, heads, _ = item
        keys = stack([k_ref[f, block(i)] for f in range(count)])
        return dot_nt(keys, rows_of(q_ref, heads, i, size))

    def second(item, raw):
        i, _, lanes = item
        before = stat_ref[i, 1:2, lanes]
        biases = [bias_ref[i, n : n + 1, lanes] for n in plan.far]
        exps, top = scores_of(plan, raw, biases, None, before)
        fade = jnp.exp2(before - top)
        total = acc_ref[i, size : size + 1, lanes] * fade
        total = total + sum(jnp.sum(part, axis=0, keepdims=True) for part in exps)
        inverse = 1.0 / total
        low_ref[i, :, lanes] = (stack(exps) * inverse).astype(BF16)
        fin_ref[i, 0:1, lanes] = jnp.exp2(stat_ref[i, 0:1, lanes] - top) * inverse
        fin_ref[i, 1:2, lanes] = fade * inverse
        fin_ref[i, 2:3, lanes] = stat_ref[i, 2:3, lanes] * (fade * inverse)
        if lanes.stop == plan.lanes:
            dv = dot_nt(low_ref[i], dot_ref[i])
            for f in range(count):
                dv_ref[f, block(i)] = dv[block(f)].astype(BF16)

    @pl.when(has_far(plan))
    def _():
        staged(plan.items(FAR_WIDE), first, second)

    @pl.when(jnp.logical_not(has_far(plan)))
    def _():
        dv_ref[...] = jnp.zeros_like(dv_ref)
        low_ref[...] = jnp.zeros_like(low_ref)
        for i in range(plan.blocks):
            inverse = 1.0 / acc_ref[i, size : size + 1, :]
            fin_ref[i, 0:1, :] = jnp.exp2(stat_ref[i, 0:1, :] - stat_ref[i, 1:2, :]) * inverse
            fin_ref[i, 1:2, :] = inverse
            fin_ref[i, 2:3, :] = stat_ref[i, 2:3, :] * inverse


def far_keys(plan, q_ref, dot_ref, v_ref, low_ref, fin_in, dk_ref, ds_ref, fin_ref):
    size = plan.size
    count = len(plan.far)

    def first(item):
        i, _, lanes = item
        values = stack([v_ref[f, block(i)] for f in range(count)])
        return dot_nn(values, dot_ref[i, :, lanes])

    def second(item, grad_w):
        i, _, lanes = item
        weights = low_ref[i, :, lanes].astype(F32)
        products = weights * grad_w
        row_dot = fin_in[i, 2:3, lanes] + jnp.sum(products, axis=0, keepdims=True)
        ds_ref[i, :, lanes] = (products - weights * row_dot).astype(BF16)
        fin_ref[i, 2:3, lanes] = row_dot
        if lanes.stop == plan.lanes:
            dk = dot_nn(ds_ref[i], rows_of(q_ref, slice(0, plan.heads), i, size)) * plan.inv_root
            for f in range(count):
                dk_ref[f, block(i)] = dk[block(f)].astype(BF16)

    fin_ref[...] = fin_in[...]

    @pl.when(has_far(plan))
    def _():
        staged(plan.items(FAR_WIDE), first, second)

    @pl.when(jnp.logical_not(has_far(plan)))
    def _():
        dk_ref[...] = jnp.zeros_like(dk_ref)
        ds_ref[...] = jnp.zeros_like(ds_ref)


def add_blocks(sums, slots, parts):
    for n, (_, b) in enumerate(slots):
        part = parts[block(n)]
        sums[b] = part if b not in sums else sums[b] + part


def scale_rows(plan, i, factor, dot_ref, fin_ref, scaled_ref):
    for heads, lanes in plan.chunks(BACK_WIDE):
        fade = fin_ref[i, factor : factor + 1, lanes]
        scaled_ref[i, :, lanes] = (dot_ref[i, :, lanes].astype(F32) * fade).astype(BF16)


def score_grads(plan, i, slots, values, factor, fin_ref, p_ref, p_at, ds_ref, ds_at, scaled_ref):
    tall = len(slots) * BLK
    for heads, lanes in plan.chunks(BACK_WIDE):
        fade = fin_ref[i, factor : factor + 1, lanes]
        shifted = dot_nn(values, scaled_ref[i, :, lanes]) - fin_ref[i, 2:3, lanes] * fade
        ds_ref[ds_at : ds_at + tall, lanes] = (p_ref[p_at : p_at + tall, lanes].astype(F32) * shifted).astype(BF16)


def prev_values(plan, dot_ref, fin_ref, p_ref, dv_ref, scaled_ref):
    sums = {}
    for i in range(plan.blocks):
        scale_rows(plan, i, 1, dot_ref, fin_ref, scaled_ref)
        part = p_ref[plan.prev_at[i] * BLK : plan.prev_at[i + 1] * BLK, :]
        add_blocks(sums, plan.prev[i], dot_nt(part, scaled_ref[i]))
    for b in range(plan.blocks):
        dv_ref[block(b)] = sums[b]


def prev_keys(plan, q_ref, v_ref, fin_ref, p_ref, scaled_ref, dk_ref, ds_ref):
    sums = {}
    for i in range(plan.blocks):
        slots = plan.prev[i]
        values = stack([v_ref[block(b)] for _, b in slots])
        at, end = plan.prev_at[i] * BLK, plan.prev_at[i + 1] * BLK
        score_grads(plan, i, slots, values, 1, fin_ref, p_ref, at, ds_ref, at, scaled_ref)
        dk = dot_nn(ds_ref[at:end, :], rows_of(q_ref, slice(0, plan.heads), i, plan.size))
        add_blocks(sums, slots, dk)
    for b in range(plan.blocks):
        dk_ref[block(b)] = sums[b] * plan.inv_root


def local_backward(
    plan, q_ref, dot_ref, k_ref, v_ref, kp_ref, kf_ref, vf_ref, fin_ref, acc_ref, low_ref, p_ref, dsp_ref, dsf_ref,
    dk_ref, dv_ref, o_hbm, dq_hbm, scaled_ref, ds_ref, o_ref, dq_ref, sems,
):
    size = plan.size
    count = len(plan.far)
    copies = []

    def send(source, target, i):
        copies.append(pltpu.make_async_copy(source.at[:, block(i)], target.at[:, block(i)], sems.at[len(copies)]))
        copies[-1].start()

    for i in range(plan.blocks):
        vt = stack([vf_ref[f, block(i)] for f in range(count)]).T
        for heads, lanes in plan.chunks(BACK_WIDE):
            out_t = acc_ref[i, :size, lanes] * fin_ref[i, 1:2, lanes] + dot_nn(vt, low_ref[i, :, lanes])
            o_ref[heads, block(i)] = out_t.astype(BF16).T.reshape(BACK_WIDE, BLK, size)
        send(o_ref, o_hbm, i)
    dk_sums, dv_sums = {}, {}
    keys_t = k_ref[...].T
    prev_t = kp_ref[...].T
    for i in range(plan.blocks):
        slots = plan.own[i]
        values = stack([v_ref[block(b)] for _, b in slots])
        at, end = plan.own_at[i] * BLK, plan.own_at[i + 1] * BLK
        scale_rows(plan, i, 0, dot_ref, fin_ref, scaled_ref)
        score_grads(plan, i, slots, values, 0, fin_ref, p_ref, at, ds_ref, at, scaled_ref)
        kt = [keys_t[:, block(b)] for _, b in slots]
        kt += [prev_t[:, block(b)] for _, b in plan.prev[i]]
        kt += [kf_ref[f, block(i)].T for f in range(count)]
        kt = stack(kt, axis=1)
        for heads, lanes in plan.chunks(BACK_WIDE):
            ds = [ds_ref[at:end, lanes]]
            if plan.prev[i]:
                ds.append(dsp_ref[plan.prev_at[i] * BLK : plan.prev_at[i + 1] * BLK, lanes])
            if count:
                ds.append(dsf_ref[i, :, lanes])
            dq_t = (dot_nn(kt, stack(ds)) * plan.inv_root).astype(BF16)
            dq_ref[heads, block(i)] = dq_t.T.reshape(BACK_WIDE, BLK, size)
        send(dq_ref, dq_hbm, i)
        add_blocks(dv_sums, slots, dot_nt(p_ref[at:end, :], scaled_ref[i]))
        add_blocks(dk_sums, slots, dot_nn(ds_ref[at:end, :], rows_of(q_ref, slice(0, plan.heads), i, size)))
    for b in range(plan.blocks):
        dk_ref[block(b)] = dk_sums[b] * plan.inv_root
        dv_ref[block(b)] = dv_sums[b]
    for copy in copies:
        copy.wait()


def finish(plan, dk_ref, dv_ref, kg_ref, vg_ref, k_hbm, v_hbm, k_out, v_out, sems):
    copies = []
    for n, (own, arrived, out, target) in enumerate(
        ((dv_ref, vg_ref, v_out, v_hbm), (dk_ref, kg_ref, k_out, k_hbm))
    ):
        out[0] = (own[...] + arrived[...].astype(F32)).astype(BF16)
        copies.append(pltpu.make_async_copy(out, target, sems.at[n]))
        copies[n].start()
    for copy in copies:
        copy.wait()


def local(queries, key_rows, value_rows, out_grad, link_mask):
    heads, rows, size = queries.shape
    blocks = rows // BLK
    plan = Plan(blocks, heads, size, lax.axis_size("ctx"))
    lanes = plan.lanes
    count = len(plan.far)

    keys, values = key_rows[0], value_rows[0]
    k_prev = shift(keys, "ctx", 1, 0)
    v_prev = shift(values, "ctx", 1, 0)
    k_far = far_rows(keys, k_prev, plan.hops)
    v_far = far_rows(values, v_prev, plan.hops)

    def array(*shape, dtype=BF16):
        return jax.ShapeDtypeStruct(shape, dtype)

    vmem = pl.BlockSpec(memory_space=pltpu.VMEM)
    smem = pl.BlockSpec(memory_space=pltpu.SMEM)
    hbm = pl.BlockSpec(memory_space=pltpu.HBM)

    def call(body, slots, matmuls, outs, operands, scratch=(), places=None, lasts=(), alias=None):
        flops = 2 * matmuls * slots * BLK * lanes * size
        return pl.pallas_call(
            functools.partial(body, plan),
            in_specs=places or [vmem] * len(operands),
            out_specs=[vmem] * (len(outs) - len(lasts)) + list(lasts),
            out_shape=outs,
            scratch_shapes=list(scratch),
            input_output_aliases=alias or {},
            compiler_params=pltpu.CompilerParams(vmem_limit_bytes=20 << 20),
            cost_estimate=pl.CostEstimate(
                flops=flops, bytes_accessed=4 * queries.size, transcendentals=slots * BLK * lanes
            ),
        )(*operands)

    n_own, n_prev, n_far = plan.own_at[-1], plan.prev_at[-1], count * blocks
    stat = array(blocks, 8, lanes, dtype=F32)
    acc = array(blocks, size + 8, lanes, dtype=F32)
    total = array(rows, size, dtype=F32)
    bias = array(blocks, 16, lanes, dtype=F32)
    grads_t = array(blocks, size, lanes)
    own_shape, prev_shape = array(n_own * BLK, lanes), array(n_prev * BLK, lanes)
    ds_shape = array(blocks, count * BLK, lanes)
    far_shape = array(count, rows, size)
    full = array(*queries.shape)
    whole = pltpu.VMEM(queries.shape, BF16)

    causal = call(causal_mask, n_own, 8, [array(BLK, lanes, dtype=F32)], ())[0]
    bias, stat_own, acc_own, p_own, grad_t = call(
        local_forward, n_own, 2,
        [bias, stat, acc, own_shape, grads_t],
        (link_mask, causal, queries, out_grad, key_rows, value_rows),
        places=[smem] + [vmem] * 5,
    )
    stat_near, acc_near, p_prev = call(
        prev_forward, n_prev, 2,
        [stat, acc, prev_shape],
        (queries, k_prev, v_prev, grad_t, bias, stat_own, acc_own),
    )
    dv_far, low_far, fin = call(
        far_scores, n_far, 2,
        [far_shape, ds_shape, stat],
        (queries, grad_t, k_far, bias, stat_near, acc_near),
    )
    dk_far, ds_far, fin = call(
        far_keys, n_far, 2,
        [far_shape, ds_shape, stat],
        (queries, grad_t, v_far, low_far, fin),
    )
    dv_prev, scaled = call(prev_values, n_prev, 1, [total, grads_t], (grad_t, fin, p_prev))
    dk_prev, ds_prev = call(prev_keys, n_prev, 2, [total, prev_shape], (queries, v_prev, fin, p_prev, scaled))
    dk_own, dv_own, output, query_grad = call(
        local_backward, n_own, 5,
        [total, total, full, full],
        (queries, grad_t, keys, values, k_prev, k_far, v_far, fin, acc_near, low_far, p_own, ds_prev, ds_far),
        scratch=[
            pltpu.VMEM(grads_t.shape, BF16), pltpu.VMEM(own_shape.shape, BF16), whole, whole, pltpu.SemaphoreType.DMA((2 * blocks,))
        ],
        lasts=(hbm, hbm),
    )

    def send_back(pending, prev):
        levels = [(1, prev)] + [(hop, pending[n].astype(F32)) for n, hop in enumerate(plan.hops)]
        arrived = None
        for n in reversed(range(len(levels))):
            hop, mine = levels[n]
            below = levels[n - 1][0] if n > 0 else 0
            running = mine if arrived is None else mine + arrived.astype(F32)
            arrived = shift(running.astype(BF16), "ctx", below - hop, hop)
        return arrived

    v_arrived = send_back(dv_far, dv_prev)
    k_arrived = send_back(dk_far, dk_prev)
    line = array(1, rows, size)
    key_grad, value_grad = call(
        finish, 1, 1, [line, line], (dk_own, dv_own, k_arrived, v_arrived),
        scratch=[pltpu.VMEM(line.shape, BF16), pltpu.VMEM(line.shape, BF16), pltpu.SemaphoreType.DMA((2,))],
        lasts=(hbm, hbm),
    )
    return output, query_grad, key_grad, value_grad


def solution(mesh):
    split = P(("groups", "head"), "ctx", None)

    return jax.shard_map(
        local,
        mesh=mesh,
        in_specs=(split, split, split, split, P(("groups", "ctx"), None)),
        out_specs=(split, split, split, split),
        check_vma=False,
    )
```

```python
import functools
import math

import jax
import jax.numpy as jnp
from jax import lax
from jax.experimental import pallas as pl
from jax.experimental.pallas import tpu as pltpu
from jax.sharding import PartitionSpec as P


BLK = 128
NOFF = 11
OWN_WIDE = 8
PREV_WIDE = 4
SCORE_WIDE = 2
KEY_WIDE = 4
BACK_WIDE = 2
NEG = -1e30
LOG2E = 1.4426950408889634
F32 = jnp.float32
BF16 = jnp.bfloat16


def shift(value, axis, steps, holders):
    count = lax.axis_size(axis)
    return lax.ppermute(value, axis, [(n, n + steps) for n in range(holders, count) if 0 <= n + steps < count])


def two_up(own, near, axis):
    count = lax.axis_size(axis)
    straight = lax.ppermute(own, axis, [(n, n + 2) for n in range(0, count - 2, 2)])
    relayed = lax.ppermute(near, axis, [(n, n + 1) for n in range(2, count - 1, 2)])
    return straight + relayed


def far_rows(own, near, hops):
    rows = [two_up(own, near, "ctx")]
    for at, hop in zip(hops, hops[1:]):
        rows.append(shift(rows[-1], "ctx", hop - at, at))
    return rows[0][None] if len(rows) == 1 else jnp.stack(rows)


def slot_table(block_count, ctx_size):
    entries = []
    for slot_id in range(NOFF):
        offset = 0 if slot_id == 0 else 2 ** (slot_id - 1)
        if offset < block_count:
            entries.append((slot_id, offset, 0))
        elif offset // block_count < ctx_size:
            entries.append((slot_id, offset, offset // block_count))
    return entries


def dot_nt(a, b):
    return lax.dot_general(a, b, (((1,), (1,)), ((), ())), preferred_element_type=F32)


def dot_nn(a, b):
    return lax.dot_general(a, b, (((1,), (0,)), ((), ())), preferred_element_type=F32)


def block(n):
    return slice(n * BLK, (n + 1) * BLK)


def stack(parts, axis=0):
    return parts[0] if len(parts) == 1 else jnp.concatenate(parts, axis=axis)


class Plan:
    def __init__(self, blocks, heads, size, ctx_size):
        self.blocks, self.heads, self.size = blocks, heads, size
        self.entries = slot_table(blocks, ctx_size)
        self.lanes = heads * BLK
        near = [(n, e[1]) for n, e in enumerate(self.entries) if e[1] <= blocks]
        self.far = [n for n, e in enumerate(self.entries) if e[1] > blocks]
        self.hops = [self.entries[n][2] for n in self.far]
        self.own = [[(n, i - o) for n, o in near if o <= i] for i in range(blocks)]
        self.prev = [[(n, i - o + blocks) for n, o in near if o > i] for i in range(blocks)]
        self.own_at = [sum(len(s) for s in self.own[:i]) for i in range(blocks + 1)]
        self.prev_at = [sum(len(s) for s in self.prev[:i]) for i in range(blocks + 1)]
        self.scale = LOG2E / math.sqrt(size)
        self.inv_root = 1.0 / math.sqrt(size)

    def chunks(self, wide):
        for first in range(0, self.heads, wide):
            yield slice(first, first + wide), slice(first * BLK, (first + wide) * BLK)

    def items(self, wide, rows=None):
        for i in range(self.blocks) if rows is None else rows:
            for heads, lanes in self.chunks(wide):
                yield i, heads, lanes


def rows_of(ref, heads, i, size):
    return ref[heads, block(i)].reshape(-1, size)


def with_ones(values_t):
    width = values_t.shape[1]
    row = lax.broadcasted_iota(jnp.int32, (16, width), 0)
    return jnp.concatenate([values_t, jnp.where(row == 0, 1.0, 0.0).astype(BF16)], axis=0)


def scores_of(plan, raw, biases, mask, top):
    parts = [raw[block(n)] for n in range(len(biases))]
    if mask is not None:
        parts[0] = parts[0] + mask
    for part, bias in zip(parts, biases):
        high = jnp.max(part, axis=0, keepdims=True) * plan.scale
        if bias is not None:
            high = high + bias
        top = high if top is None else jnp.maximum(top, high)
    exps = []
    for part, bias in zip(parts, biases):
        base = top if bias is None else top - bias
        exps.append(jnp.exp2(part * plan.scale - base))
    return exps, top


def staged(items, *stages):
    items = list(items)
    held = {}
    for step in range(len(items) + len(stages) - 1):
        for k, stage in enumerate(stages):
            n = step - k
            if 0 <= n < len(items):
                held[n] = stage(items[n], *held.pop(n, ()))


def causal_mask(plan, mask_ref):
    key = lax.broadcasted_iota(jnp.int32, mask_ref.shape, 0)
    row = lax.broadcasted_iota(jnp.int32, mask_ref.shape, 1)
    mask_ref[...] = jnp.where(key <= lax.rem(row, BLK), 0.0, NEG)


def local_forward(
    plan, link_ref, causal_ref, q_ref, do_ref, k_ref, v_ref, bias_ref, stat_ref, acc_ref, p_ref, dot_ref, qt_ref
):
    first_block = lax.axis_index("ctx") * plan.blocks
    scalars = []
    for i in range(plan.blocks):
        scalars.append([])
        for n, (slot_id, offset, _) in enumerate(plan.entries):
            live = (link_ref[i, slot_id] == 1) & (first_block + i >= offset)
            scalars[i].append(jnp.where(live, 0.0, NEG).astype(F32))
            bias_ref[i, n : n + 1, :] = jnp.full((1, plan.lanes), scalars[i][n], F32)
    values_t = with_ones(v_ref[0].T)
    size = plan.size

    def first(item):
        i, heads, _ = item
        keys = stack([k_ref[0, block(b)] for _, b in plan.own[i]])
        return (dot_nt(keys, rows_of(q_ref, heads, i, size)),)

    def second(item, raw):
        i, _, lanes = item
        slots = plan.own[i]
        biases = [scalars[i][n] if plan.entries[n][1] > 0 else None for n, _ in slots]
        at = plan.own_at[i] * BLK
        exps, top = scores_of(plan, raw, biases, causal_ref[:, lanes], None)
        low = stack([part.astype(BF16) for part in exps])
        p_ref[at : at + low.shape[0], lanes] = low
        stat_ref[i, 0:1, lanes] = top
        return (low,)

    def third(item, low):
        i, heads, lanes = item
        vt = stack([values_t[:, block(b)] for _, b in plan.own[i]], axis=1)
        acc_ref[i, :, lanes] = dot_nn(vt, low)[: size + 8]
        dot_ref[i, :, lanes] = rows_of(do_ref, heads, i, size).T
        qt_ref[i, :, lanes] = rows_of(q_ref, heads, i, size).T
        return ()

    staged(plan.items(OWN_WIDE), first, second, third)


def prev_forward(plan, q_ref, k_ref, v_ref, dot_ref, bias_ref, stat_in, acc_in, stat_ref, acc_ref, p_ref):
    size = plan.size
    values_t = with_ones(v_ref[...].T)

    def first(item):
        i, heads, _ = item
        keys = stack([k_ref[block(b)] for _, b in plan.prev[i]])
        return (dot_nt(keys, rows_of(q_ref, heads, i, size)),)

    def second(item, raw):
        i, _, lanes = item
        slots = plan.prev[i]
        at = plan.prev_at[i] * BLK
        before = stat_in[i, 0:1, lanes]
        biases = [bias_ref[i, n : n + 1, lanes] for n, _ in slots]
        exps, top = scores_of(plan, raw, biases, None, before)
        low = stack([part.astype(BF16) for part in exps])
        p_ref[at : at + low.shape[0], lanes] = low
        return low, before, top

    def third(item, low, before, top):
        i, _, lanes = item
        vt = stack([values_t[:, block(b)] for _, b in plan.prev[i]], axis=1)
        acc = acc_in[i, :, lanes] * jnp.exp2(before - top) + dot_nn(vt, low)[: size + 8]
        acc_ref[i, :, lanes] = acc
        stat_ref[i, 0:1, lanes] = before
        stat_ref[i, 1:2, lanes] = top
        stat_ref[i, 2:3, lanes] = jnp.sum(acc[:size] * dot_ref[i, :, lanes].astype(F32), axis=0, keepdims=True)
        return ()

    staged(plan.items(PREV_WIDE), first, second, third)


def has_far(plan):
    return (lax.axis_index("ctx") + 1) * plan.blocks > plan.entries[plan.far[0]][1]


def far_scores(plan, q_ref, dot_ref, k_ref, bias_ref, stat_ref, acc_ref, dv_ref, low_ref, fin_ref):
    size = plan.size
    count = len(plan.far)

    def first(item):
        i, heads, _ = item
        keys = stack([k_ref[f, block(i)] for f in range(count)])
        return (dot_nt(keys, rows_of(q_ref, heads, i, size)),)

    def second(item, raw):
        i, _, lanes = item
        before = stat_ref[i, 1:2, lanes]
        biases = [bias_ref[i, n : n + 1, lanes] for n in plan.far]
        exps, top = scores_of(plan, raw, biases, None, before)
        fade = jnp.exp2(before - top)
        total = acc_ref[i, size : size + 1, lanes] * fade
        total = total + sum(jnp.sum(part, axis=0, keepdims=True) for part in exps)
        inverse = 1.0 / total
        low_ref[i, :, lanes] = (stack(exps) * inverse).astype(BF16)
        fin_ref[i, 0:1, lanes] = jnp.exp2(stat_ref[i, 0:1, lanes] - top) * inverse
        fin_ref[i, 1:2, lanes] = fade * inverse
        fin_ref[i, 2:3, lanes] = stat_ref[i, 2:3, lanes] * (fade * inverse)
        return ()

    def third(item):
        i, _, lanes = item
        if lanes.stop == plan.lanes:
            dv = dot_nt(low_ref[i], dot_ref[i])
            for f in range(count):
                dv_ref[f, block(i)] = dv[block(f)].astype(BF16)
        return ()

    @pl.when(has_far(plan))
    def _():
        staged(plan.items(SCORE_WIDE), first, second, third)

    @pl.when(jnp.logical_not(has_far(plan)))
    def _():
        dv_ref[...] = jnp.zeros_like(dv_ref)
        low_ref[...] = jnp.zeros_like(low_ref)
        for i in range(plan.blocks):
            inverse = 1.0 / acc_ref[i, size : size + 1, :]
            fin_ref[i, 0:1, :] = jnp.exp2(stat_ref[i, 0:1, :] - stat_ref[i, 1:2, :]) * inverse
            fin_ref[i, 1:2, :] = inverse
            fin_ref[i, 2:3, :] = stat_ref[i, 2:3, :] * inverse


def far_keys(plan, qt_ref, dot_ref, v_ref, low_ref, fin_in, dk_ref, ds_ref, fin_ref):
    count = len(plan.far)

    def first(item):
        i, _, lanes = item
        values = stack([v_ref[f, block(i)] for f in range(count)])
        return (dot_nn(values, dot_ref[i, :, lanes]),)

    def second(item, grad_w):
        i, _, lanes = item
        weights = low_ref[i, :, lanes].astype(F32)
        products = weights * grad_w
        row_dot = fin_in[i, 2:3, lanes] + jnp.sum(products, axis=0, keepdims=True)
        ds_ref[i, :, lanes] = (products - weights * row_dot).astype(BF16)
        fin_ref[i, 2:3, lanes] = row_dot
        return ()

    def third(item):
        i, _, lanes = item
        if lanes.stop == plan.lanes:
            dk = dot_nt(ds_ref[i], qt_ref[i]) * plan.inv_root
            for f in range(count):
                dk_ref[f, block(i)] = dk[block(f)].astype(BF16)
        return ()

    fin_ref[...] = fin_in[...]

    @pl.when(has_far(plan))
    def _():
        staged(plan.items(KEY_WIDE), first, second, third)

    @pl.when(jnp.logical_not(has_far(plan)))
    def _():
        dk_ref[...] = jnp.zeros_like(dk_ref)
        ds_ref[...] = jnp.zeros_like(ds_ref)


def add_blocks(sums, slots, parts):
    for n, (_, b) in enumerate(slots):
        part = parts[block(n)]
        sums[b] = part if b not in sums else sums[b] + part


def scale_rows(plan, i, factor, dot_ref, fin_ref, scaled_ref):
    for heads, lanes in plan.chunks(BACK_WIDE):
        fade = fin_ref[i, factor : factor + 1, lanes]
        scaled_ref[i, :, lanes] = (dot_ref[i, :, lanes].astype(F32) * fade).astype(BF16)


def score_grads(plan, i, slots, values, factor, fin_ref, p_ref, p_at, ds_ref, ds_at, scaled_ref):
    tall = len(slots) * BLK
    for heads, lanes in plan.chunks(BACK_WIDE):
        fade = fin_ref[i, factor : factor + 1, lanes]
        shifted = dot_nn(values, scaled_ref[i, :, lanes]) - fin_ref[i, 2:3, lanes] * fade
        ds_ref[ds_at : ds_at + tall, lanes] = (p_ref[p_at : p_at + tall, lanes].astype(F32) * shifted).astype(BF16)


def prev_values(plan, dot_ref, fin_ref, p_ref, dv_ref, scaled_ref):
    sums = {}
    for i in range(plan.blocks):
        scale_rows(plan, i, 1, dot_ref, fin_ref, scaled_ref)
        part = p_ref[plan.prev_at[i] * BLK : plan.prev_at[i + 1] * BLK, :]
        add_blocks(sums, plan.prev[i], dot_nt(part, scaled_ref[i]))
    for b in range(plan.blocks):
        dv_ref[block(b)] = sums[b]


def prev_keys(plan, qt_ref, v_ref, fin_ref, p_ref, scaled_ref, dk_ref, ds_ref):
    sums = {}
    for i in range(plan.blocks):
        slots = plan.prev[i]
        values = stack([v_ref[block(b)] for _, b in slots])
        at, end = plan.prev_at[i] * BLK, plan.prev_at[i + 1] * BLK
        score_grads(plan, i, slots, values, 1, fin_ref, p_ref, at, ds_ref, at, scaled_ref)
        dk = dot_nt(ds_ref[at:end, :], qt_ref[i])
        add_blocks(sums, slots, dk)
    for b in range(plan.blocks):
        dk_ref[block(b)] = sums[b] * plan.inv_root


def local_backward(
    plan, qt_ref, dot_ref, k_ref, v_ref, kp_ref, kf_ref, vf_ref, fin_ref, acc_ref, low_ref, p_ref, dsp_ref, dsf_ref,
    dk_ref, dv_ref, o_hbm, dq_hbm, scaled_ref, ds_ref, o_ref, dq_ref, sems,
):
    size = plan.size
    count = len(plan.far)
    copies = []

    def send(source, target, i):
        copies.append(pltpu.make_async_copy(source.at[:, block(i)], target.at[:, block(i)], sems.at[len(copies)]))
        copies[-1].start()

    for i in range(plan.blocks):
        vt = stack([vf_ref[f, block(i)] for f in range(count)]).T
        for heads, lanes in plan.chunks(BACK_WIDE):
            out_t = acc_ref[i, :size, lanes] * fin_ref[i, 1:2, lanes] + dot_nn(vt, low_ref[i, :, lanes])
            o_ref[heads, block(i)] = out_t.astype(BF16).T.reshape(BACK_WIDE, BLK, size)
        send(o_ref, o_hbm, i)
    dk_sums, dv_sums = {}, {}
    keys_t = k_ref[...].T
    prev_t = kp_ref[...].T
    for i in range(plan.blocks):
        slots = plan.own[i]
        values = stack([v_ref[block(b)] for _, b in slots])
        at, end = plan.own_at[i] * BLK, plan.own_at[i + 1] * BLK
        scale_rows(plan, i, 0, dot_ref, fin_ref, scaled_ref)
        score_grads(plan, i, slots, values, 0, fin_ref, p_ref, at, ds_ref, at, scaled_ref)
        kt = [keys_t[:, block(b)] for _, b in slots]
        kt += [prev_t[:, block(b)] for _, b in plan.prev[i]]
        kt += [kf_ref[f, block(i)].T for f in range(count)]
        kt = stack(kt, axis=1)
        for heads, lanes in plan.chunks(BACK_WIDE):
            ds = [ds_ref[at:end, lanes]]
            if plan.prev[i]:
                ds.append(dsp_ref[plan.prev_at[i] * BLK : plan.prev_at[i + 1] * BLK, lanes])
            if count:
                ds.append(dsf_ref[i, :, lanes])
            dq_t = (dot_nn(kt, stack(ds)) * plan.inv_root).astype(BF16)
            dq_ref[heads, block(i)] = dq_t.T.reshape(BACK_WIDE, BLK, size)
        send(dq_ref, dq_hbm, i)
    for i in range(plan.blocks):
        at, end = plan.own_at[i] * BLK, plan.own_at[i + 1] * BLK
        add_blocks(dv_sums, plan.own[i], dot_nt(p_ref[at:end, :], scaled_ref[i]))
        add_blocks(dk_sums, plan.own[i], dot_nt(ds_ref[at:end, :], qt_ref[i]))
    for b in range(plan.blocks):
        dk_ref[block(b)] = dk_sums[b] * plan.inv_root
        dv_ref[block(b)] = dv_sums[b]
    for copy in copies:
        copy.wait()


def finish(plan, dk_ref, dv_ref, kg_ref, vg_ref, k_hbm, v_hbm, k_out, v_out, sems):
    copies = []
    for n, (own, arrived, out, target) in enumerate(
        ((dv_ref, vg_ref, v_out, v_hbm), (dk_ref, kg_ref, k_out, k_hbm))
    ):
        out[0] = (own[...] + arrived[...].astype(F32)).astype(BF16)
        copies.append(pltpu.make_async_copy(out, target, sems.at[n]))
        copies[n].start()
    for copy in copies:
        copy.wait()


def local(queries, key_rows, value_rows, out_grad, link_mask):
    heads, rows, size = queries.shape
    blocks = rows // BLK
    plan = Plan(blocks, heads, size, lax.axis_size("ctx"))
    lanes = plan.lanes
    count = len(plan.far)

    keys, values = key_rows[0], value_rows[0]
    k_prev = shift(keys, "ctx", 1, 0)
    v_prev = shift(values, "ctx", 1, 0)
    k_far = far_rows(keys, k_prev, plan.hops)
    v_far = far_rows(values, v_prev, plan.hops)

    def array(*shape, dtype=BF16):
        return jax.ShapeDtypeStruct(shape, dtype)

    vmem = pl.BlockSpec(memory_space=pltpu.VMEM)
    smem = pl.BlockSpec(memory_space=pltpu.SMEM)
    hbm = pl.BlockSpec(memory_space=pltpu.HBM)

    def call(body, slots, matmuls, outs, operands, scratch=(), places=None, lasts=(), alias=None):
        flops = 2 * matmuls * slots * BLK * lanes * size
        return pl.pallas_call(
            functools.partial(body, plan),
            in_specs=places or [vmem] * len(operands),
            out_specs=[vmem] * (len(outs) - len(lasts)) + list(lasts),
            out_shape=outs,
            scratch_shapes=list(scratch),
            input_output_aliases=alias or {},
            compiler_params=pltpu.CompilerParams(vmem_limit_bytes=20 << 20),
            cost_estimate=pl.CostEstimate(
                flops=flops, bytes_accessed=4 * queries.size, transcendentals=slots * BLK * lanes
            ),
        )(*operands)

    n_own, n_prev, n_far = plan.own_at[-1], plan.prev_at[-1], count * blocks
    stat = array(blocks, 8, lanes, dtype=F32)
    acc = array(blocks, size + 8, lanes, dtype=F32)
    total = array(rows, size, dtype=F32)
    bias = array(blocks, 16, lanes, dtype=F32)
    grads_t = array(blocks, size, lanes)
    own_shape, prev_shape = array(n_own * BLK, lanes), array(n_prev * BLK, lanes)
    ds_shape = array(blocks, count * BLK, lanes)
    far_shape = array(count, rows, size)
    full = array(*queries.shape)
    whole = pltpu.VMEM(queries.shape, BF16)

    causal = call(causal_mask, n_own, 8, [array(BLK, lanes, dtype=F32)], ())[0]
    bias, stat_own, acc_own, p_own, grad_t, query_t = call(
        local_forward, n_own, 2,
        [bias, stat, acc, own_shape, grads_t, grads_t],
        (link_mask, causal, queries, out_grad, key_rows, value_rows),
        places=[smem] + [vmem] * 5,
    )
    stat_near, acc_near, p_prev = call(
        prev_forward, n_prev, 2,
        [stat, acc, prev_shape],
        (queries, k_prev, v_prev, grad_t, bias, stat_own, acc_own),
    )
    dv_far, low_far, fin = call(
        far_scores, n_far, 2,
        [far_shape, ds_shape, stat],
        (queries, grad_t, k_far, bias, stat_near, acc_near),
    )
    dk_far, ds_far, fin = call(
        far_keys, n_far, 2,
        [far_shape, ds_shape, stat],
        (query_t, grad_t, v_far, low_far, fin),
    )
    dv_prev, scaled = call(prev_values, n_prev, 1, [total, grads_t], (grad_t, fin, p_prev))
    dk_prev, ds_prev = call(prev_keys, n_prev, 2, [total, prev_shape], (query_t, v_prev, fin, p_prev, scaled))
    dk_own, dv_own, output, query_grad = call(
        local_backward, n_own, 5,
        [total, total, full, full],
        (query_t, grad_t, keys, values, k_prev, k_far, v_far, fin, acc_near, low_far, p_own, ds_prev, ds_far),
        scratch=[
            pltpu.VMEM(grads_t.shape, BF16), pltpu.VMEM(own_shape.shape, BF16), whole, whole, pltpu.SemaphoreType.DMA((2 * blocks,))
        ],
        lasts=(hbm, hbm),
    )

    def send_back(pending, prev):
        levels = [(1, prev)] + [(hop, pending[n].astype(F32)) for n, hop in enumerate(plan.hops)]
        arrived = None
        for n in reversed(range(len(levels))):
            hop, mine = levels[n]
            below = levels[n - 1][0] if n > 0 else 0
            running = mine if arrived is None else mine + arrived.astype(F32)
            arrived = shift(running.astype(BF16), "ctx", below - hop, hop)
        return arrived

    v_arrived = send_back(dv_far, dv_prev)
    k_arrived = send_back(dk_far, dk_prev)
    line = array(1, rows, size)
    key_grad, value_grad = call(
        finish, 1, 1, [line, line], (dk_own, dv_own, k_arrived, v_arrived),
        scratch=[pltpu.VMEM(line.shape, BF16), pltpu.VMEM(line.shape, BF16), pltpu.SemaphoreType.DMA((2,))],
        lasts=(hbm, hbm),
    )
    return output, query_grad, key_grad, value_grad


def solution(mesh):
    split = P(("groups", "head"), "ctx", None)

    return jax.shard_map(
        local,
        mesh=mesh,
        in_specs=(split, split, split, split, P(("groups", "ctx"), None)),
        out_specs=(split, split, split, split),
        check_vma=False,
    )
```

```python
import functools
import math

import jax
import jax.numpy as jnp
from jax import lax
from jax.experimental import pallas as pl
from jax.experimental.pallas import tpu as pltpu
from jax.sharding import PartitionSpec as P


BLK = 128
NOFF = 11
OWN_WIDE = 8
PREV_WIDE = 4
SCORE_WIDE = 2
KEY_WIDE = 4
BACK_WIDE = 2
NEG = -1e30
LOG2E = 1.4426950408889634
F32 = jnp.float32
BF16 = jnp.bfloat16


def shift(value, axis, steps, holders):
    count = lax.axis_size(axis)
    return lax.ppermute(value, axis, [(n, n + steps) for n in range(holders, count) if 0 <= n + steps < count])


def two_up(own, near, axis):
    count = lax.axis_size(axis)
    straight = lax.ppermute(own, axis, [(n, n + 2) for n in range(0, count - 2, 2)])
    relayed = lax.ppermute(near, axis, [(n, n + 1) for n in range(2, count - 1, 2)])
    return straight + relayed


def far_rows(own, near, hops):
    rows = [two_up(own, near, "ctx")]
    for at, hop in zip(hops, hops[1:]):
        rows.append(shift(rows[-1], "ctx", hop - at, at))
    return rows[0][None] if len(rows) == 1 else jnp.stack(rows)


def slot_table(block_count, ctx_size):
    entries = []
    for slot_id in range(NOFF):
        offset = 0 if slot_id == 0 else 2 ** (slot_id - 1)
        if offset < block_count:
            entries.append((slot_id, offset, 0))
        elif offset // block_count < ctx_size:
            entries.append((slot_id, offset, offset // block_count))
    return entries


def dot_nt(a, b):
    return lax.dot_general(a, b, (((1,), (1,)), ((), ())), preferred_element_type=F32)


def dot_nn(a, b):
    return lax.dot_general(a, b, (((1,), (0,)), ((), ())), preferred_element_type=F32)


def block(n):
    return slice(n * BLK, (n + 1) * BLK)


def stack(parts, axis=0):
    return parts[0] if len(parts) == 1 else jnp.concatenate(parts, axis=axis)


class Plan:
    def __init__(self, blocks, heads, size, ctx_size):
        self.blocks, self.heads, self.size = blocks, heads, size
        self.entries = slot_table(blocks, ctx_size)
        self.lanes = heads * BLK
        near = [(n, e[1]) for n, e in enumerate(self.entries) if e[1] <= blocks]
        self.far = [n for n, e in enumerate(self.entries) if e[1] > blocks]
        self.hops = [self.entries[n][2] for n in self.far]
        self.own = [[(n, i - o) for n, o in near if o <= i] for i in range(blocks)]
        self.prev = [[(n, i - o + blocks) for n, o in near if o > i] for i in range(blocks)]
        self.own_at = [sum(len(s) for s in self.own[:i]) for i in range(blocks + 1)]
        self.prev_at = [sum(len(s) for s in self.prev[:i]) for i in range(blocks + 1)]
        self.scale = LOG2E / math.sqrt(size)
        self.inv_root = 1.0 / math.sqrt(size)

    def chunks(self, wide):
        for first in range(0, self.heads, wide):
            yield slice(first, first + wide), slice(first * BLK, (first + wide) * BLK)

    def items(self, wide, rows=None):
        for i in range(self.blocks) if rows is None else rows:
            for heads, lanes in self.chunks(wide):
                yield i, heads, lanes


def rows_of(ref, heads, i, size):
    return ref[heads, block(i)].reshape(-1, size)


def with_ones(values_t):
    width = values_t.shape[1]
    row = lax.broadcasted_iota(jnp.int32, (16, width), 0)
    return jnp.concatenate([values_t, jnp.where(row == 0, 1.0, 0.0).astype(BF16)], axis=0)


def scores_of(plan, raw, biases, mask, top):
    parts = [raw[block(n)] for n in range(len(biases))]
    if mask is not None:
        parts[0] = parts[0] + mask
    for part, bias in zip(parts, biases):
        high = jnp.max(part, axis=0, keepdims=True) * plan.scale
        if bias is not None:
            high = high + bias
        top = high if top is None else jnp.maximum(top, high)
    exps = []
    for part, bias in zip(parts, biases):
        base = top if bias is None else top - bias
        exps.append(jnp.exp2(part * plan.scale - base))
    return exps, top


def staged(items, *stages):
    items = list(items)
    held = {}
    for step in range(len(items) + len(stages) - 1):
        for k, stage in enumerate(stages):
            n = step - k
            if 0 <= n < len(items):
                held[n] = stage(items[n], *held.pop(n, ()))


def causal_mask(plan, mask_ref):
    key = lax.broadcasted_iota(jnp.int32, mask_ref.shape, 0)
    row = lax.broadcasted_iota(jnp.int32, mask_ref.shape, 1)
    mask_ref[...] = jnp.where(key <= lax.rem(row, BLK), 0.0, NEG)


def local_forward(
    plan, link_ref, causal_ref, q_ref, do_ref, k_ref, v_ref, bias_ref, stat_ref, acc_ref, p_ref, dot_ref, qt_ref
):
    first_block = lax.axis_index("ctx") * plan.blocks
    for i in range(plan.blocks):
        for n, (slot_id, offset, _) in enumerate(plan.entries):
            dead = jnp.where(link_ref[i : i + 1, slot_id : slot_id + 1] == 1, 0.0, NEG).astype(F32)
            late = jnp.where(first_block + i >= offset, 0.0, NEG).astype(F32)
            bias_ref[i, n : n + 1, :] = jnp.broadcast_to(dead + late, (1, plan.lanes))
    values_t = with_ones(v_ref[0].T)
    size = plan.size

    def first(item):
        i, heads, _ = item
        keys = stack([k_ref[0, block(b)] for _, b in plan.own[i]])
        return (dot_nt(keys, rows_of(q_ref, heads, i, size)),)

    def second(item, raw):
        i, _, lanes = item
        slots = plan.own[i]
        biases = [bias_ref[i, n : n + 1, lanes] if plan.entries[n][1] > 0 else None for n, _ in slots]
        at = plan.own_at[i] * BLK
        exps, top = scores_of(plan, raw, biases, causal_ref[:, lanes], None)
        low = stack([part.astype(BF16) for part in exps])
        p_ref[at : at + low.shape[0], lanes] = low
        stat_ref[i, 0:1, lanes] = top
        return (low,)

    def third(item, low):
        i, heads, lanes = item
        vt = stack([values_t[:, block(b)] for _, b in plan.own[i]], axis=1)
        acc_ref[i, :, lanes] = dot_nn(vt, low)[: size + 8]
        dot_ref[i, :, lanes] = rows_of(do_ref, heads, i, size).T
        qt_ref[i, :, lanes] = rows_of(q_ref, heads, i, size).T
        return ()

    staged(plan.items(OWN_WIDE), first, second, third)


def prev_forward(plan, q_ref, k_ref, v_ref, dot_ref, bias_ref, stat_in, acc_in, stat_ref, acc_ref, p_ref):
    size = plan.size
    values_t = with_ones(v_ref[...].T)

    def first(item):
        i, heads, _ = item
        keys = stack([k_ref[block(b)] for _, b in plan.prev[i]])
        return (dot_nt(keys, rows_of(q_ref, heads, i, size)),)

    def second(item, raw):
        i, _, lanes = item
        slots = plan.prev[i]
        at = plan.prev_at[i] * BLK
        before = stat_in[i, 0:1, lanes]
        biases = [bias_ref[i, n : n + 1, lanes] for n, _ in slots]
        exps, top = scores_of(plan, raw, biases, None, before)
        low = stack([part.astype(BF16) for part in exps])
        p_ref[at : at + low.shape[0], lanes] = low
        return low, before, top

    def third(item, low, before, top):
        i, _, lanes = item
        vt = stack([values_t[:, block(b)] for _, b in plan.prev[i]], axis=1)
        acc = acc_in[i, :, lanes] * jnp.exp2(before - top) + dot_nn(vt, low)[: size + 8]
        acc_ref[i, :, lanes] = acc
        stat_ref[i, 0:1, lanes] = before
        stat_ref[i, 1:2, lanes] = top
        stat_ref[i, 2:3, lanes] = jnp.sum(acc[:size] * dot_ref[i, :, lanes].astype(F32), axis=0, keepdims=True)
        return ()

    staged(plan.items(PREV_WIDE), first, second, third)


def has_far(plan):
    return (lax.axis_index("ctx") + 1) * plan.blocks > plan.entries[plan.far[0]][1]


def far_scores(plan, q_ref, dot_ref, k_ref, bias_ref, stat_ref, acc_ref, dv_ref, low_ref, fin_ref):
    size = plan.size
    count = len(plan.far)

    def first(item):
        i, heads, _ = item
        keys = stack([k_ref[f, block(i)] for f in range(count)])
        return (dot_nt(keys, rows_of(q_ref, heads, i, size)),)

    def second(item, raw):
        i, _, lanes = item
        before = stat_ref[i, 1:2, lanes]
        biases = [bias_ref[i, n : n + 1, lanes] for n in plan.far]
        exps, top = scores_of(plan, raw, biases, None, before)
        fade = jnp.exp2(before - top)
        total = acc_ref[i, size : size + 1, lanes] * fade
        total = total + sum(jnp.sum(part, axis=0, keepdims=True) for part in exps)
        inverse = 1.0 / total
        low_ref[i, :, lanes] = (stack(exps) * inverse).astype(BF16)
        fin_ref[i, 0:1, lanes] = jnp.exp2(stat_ref[i, 0:1, lanes] - top) * inverse
        fin_ref[i, 1:2, lanes] = fade * inverse
        fin_ref[i, 2:3, lanes] = stat_ref[i, 2:3, lanes] * (fade * inverse)
        return ()

    def third(item):
        i, _, lanes = item
        if lanes.stop == plan.lanes:
            dv = dot_nt(low_ref[i], dot_ref[i])
            for f in range(count):
                dv_ref[f, block(i)] = dv[block(f)].astype(BF16)
        return ()

    @pl.when(has_far(plan))
    def _():
        staged(plan.items(SCORE_WIDE), first, second, third)

    @pl.when(jnp.logical_not(has_far(plan)))
    def _():
        dv_ref[...] = jnp.zeros_like(dv_ref)
        low_ref[...] = jnp.zeros_like(low_ref)
        for i in range(plan.blocks):
            inverse = 1.0 / acc_ref[i, size : size + 1, :]
            fin_ref[i, 0:1, :] = jnp.exp2(stat_ref[i, 0:1, :] - stat_ref[i, 1:2, :]) * inverse
            fin_ref[i, 1:2, :] = inverse
            fin_ref[i, 2:3, :] = stat_ref[i, 2:3, :] * inverse


def far_keys(plan, qt_ref, dot_ref, v_ref, low_ref, fin_in, dk_ref, ds_ref, fin_ref):
    count = len(plan.far)

    def first(item):
        i, _, lanes = item
        values = stack([v_ref[f, block(i)] for f in range(count)])
        return (dot_nn(values, dot_ref[i, :, lanes]),)

    def second(item, grad_w):
        i, _, lanes = item
        weights = low_ref[i, :, lanes].astype(F32)
        products = weights * grad_w
        row_dot = fin_in[i, 2:3, lanes] + jnp.sum(products, axis=0, keepdims=True)
        ds_ref[i, :, lanes] = (products - weights * row_dot).astype(BF16)
        fin_ref[i, 2:3, lanes] = row_dot
        return ()

    def third(item):
        i, _, lanes = item
        if lanes.stop == plan.lanes:
            dk = dot_nt(ds_ref[i], qt_ref[i]) * plan.inv_root
            for f in range(count):
                dk_ref[f, block(i)] = dk[block(f)].astype(BF16)
        return ()

    fin_ref[...] = fin_in[...]

    @pl.when(has_far(plan))
    def _():
        staged(plan.items(KEY_WIDE), first, second, third)

    @pl.when(jnp.logical_not(has_far(plan)))
    def _():
        dk_ref[...] = jnp.zeros_like(dk_ref)
        ds_ref[...] = jnp.zeros_like(ds_ref)


def add_blocks(sums, slots, parts):
    for n, (_, b) in enumerate(slots):
        part = parts[block(n)]
        sums[b] = part if b not in sums else sums[b] + part


def scale_rows(plan, i, factor, dot_ref, fin_ref, scaled_ref):
    for heads, lanes in plan.chunks(BACK_WIDE):
        fade = fin_ref[i, factor : factor + 1, lanes]
        scaled_ref[i, :, lanes] = (dot_ref[i, :, lanes].astype(F32) * fade).astype(BF16)


def score_grads(plan, i, slots, values, factor, fin_ref, p_ref, p_at, ds_ref, ds_at, scaled_ref):
    tall = len(slots) * BLK
    for heads, lanes in plan.chunks(BACK_WIDE):
        fade = fin_ref[i, factor : factor + 1, lanes]
        shifted = dot_nn(values, scaled_ref[i, :, lanes]) - fin_ref[i, 2:3, lanes] * fade
        ds_ref[ds_at : ds_at + tall, lanes] = (p_ref[p_at : p_at + tall, lanes].astype(F32) * shifted).astype(BF16)


def prev_values(plan, dot_ref, fin_ref, p_ref, dv_ref, scaled_ref):
    sums = {}
    for i in range(plan.blocks):
        scale_rows(plan, i, 1, dot_ref, fin_ref, scaled_ref)
        part = p_ref[plan.prev_at[i] * BLK : plan.prev_at[i + 1] * BLK, :]
        add_blocks(sums, plan.prev[i], dot_nt(part, scaled_ref[i]))
    for b in range(plan.blocks):
        dv_ref[block(b)] = sums[b]


def prev_keys(plan, qt_ref, v_ref, fin_ref, p_ref, scaled_ref, dk_ref, ds_ref):
    sums = {}
    for i in range(plan.blocks):
        slots = plan.prev[i]
        values = stack([v_ref[block(b)] for _, b in slots])
        at, end = plan.prev_at[i] * BLK, plan.prev_at[i + 1] * BLK
        score_grads(plan, i, slots, values, 1, fin_ref, p_ref, at, ds_ref, at, scaled_ref)
        dk = dot_nt(ds_ref[at:end, :], qt_ref[i])
        add_blocks(sums, slots, dk)
    for b in range(plan.blocks):
        dk_ref[block(b)] = sums[b] * plan.inv_root


def local_backward(
    plan, qt_ref, dot_ref, k_ref, v_ref, kp_ref, kf_ref, vf_ref, fin_ref, acc_ref, low_ref, p_ref, dsp_ref, dsf_ref,
    dk_ref, dv_ref, o_hbm, dq_hbm, scaled_ref, ds_ref, o_ref, dq_ref, sems,
):
    size = plan.size
    count = len(plan.far)
    copies = []

    def send(source, target, i):
        copies.append(pltpu.make_async_copy(source.at[:, block(i)], target.at[:, block(i)], sems.at[len(copies)]))
        copies[-1].start()

    for i in range(plan.blocks):
        vt = stack([vf_ref[f, block(i)] for f in range(count)]).T
        for heads, lanes in plan.chunks(BACK_WIDE):
            out_t = acc_ref[i, :size, lanes] * fin_ref[i, 1:2, lanes] + dot_nn(vt, low_ref[i, :, lanes])
            o_ref[heads, block(i)] = out_t.astype(BF16).T.reshape(BACK_WIDE, BLK, size)
        send(o_ref, o_hbm, i)
    dk_sums, dv_sums = {}, {}
    keys_t = k_ref[...].T
    prev_t = kp_ref[...].T
    for i in range(plan.blocks):
        slots = plan.own[i]
        values = stack([v_ref[block(b)] for _, b in slots])
        at, end = plan.own_at[i] * BLK, plan.own_at[i + 1] * BLK
        scale_rows(plan, i, 0, dot_ref, fin_ref, scaled_ref)
        score_grads(plan, i, slots, values, 0, fin_ref, p_ref, at, ds_ref, at, scaled_ref)
        kt = [keys_t[:, block(b)] for _, b in slots]
        kt += [prev_t[:, block(b)] for _, b in plan.prev[i]]
        kt += [kf_ref[f, block(i)].T for f in range(count)]
        kt = stack(kt, axis=1)
        for heads, lanes in plan.chunks(BACK_WIDE):
            ds = [ds_ref[at:end, lanes]]
            if plan.prev[i]:
                ds.append(dsp_ref[plan.prev_at[i] * BLK : plan.prev_at[i + 1] * BLK, lanes])
            if count:
                ds.append(dsf_ref[i, :, lanes])
            dq_t = (dot_nn(kt, stack(ds)) * plan.inv_root).astype(BF16)
            dq_ref[heads, block(i)] = dq_t.T.reshape(BACK_WIDE, BLK, size)
        send(dq_ref, dq_hbm, i)
    for i in range(plan.blocks):
        at, end = plan.own_at[i] * BLK, plan.own_at[i + 1] * BLK
        add_blocks(dv_sums, plan.own[i], dot_nt(p_ref[at:end, :], scaled_ref[i]))
        add_blocks(dk_sums, plan.own[i], dot_nt(ds_ref[at:end, :], qt_ref[i]))
    for b in range(plan.blocks):
        dk_ref[block(b)] = dk_sums[b] * plan.inv_root
        dv_ref[block(b)] = dv_sums[b]
    for copy in copies:
        copy.wait()


def finish(plan, dk_ref, dv_ref, kg_ref, vg_ref, k_hbm, v_hbm, k_out, v_out, sems):
    copies = []
    for n, (own, arrived, out, target) in enumerate(
        ((dv_ref, vg_ref, v_out, v_hbm), (dk_ref, kg_ref, k_out, k_hbm))
    ):
        out[0] = (own[...] + arrived[...].astype(F32)).astype(BF16)
        copies.append(pltpu.make_async_copy(out, target, sems.at[n]))
        copies[n].start()
    for copy in copies:
        copy.wait()


def local(queries, key_rows, value_rows, out_grad, link_mask):
    heads, rows, size = queries.shape
    blocks = rows // BLK
    plan = Plan(blocks, heads, size, lax.axis_size("ctx"))
    lanes = plan.lanes
    count = len(plan.far)

    keys, values = key_rows[0], value_rows[0]
    k_prev = shift(keys, "ctx", 1, 0)
    v_prev = shift(values, "ctx", 1, 0)
    k_far = far_rows(keys, k_prev, plan.hops)
    v_far = far_rows(values, v_prev, plan.hops)

    def array(*shape, dtype=BF16):
        return jax.ShapeDtypeStruct(shape, dtype)

    vmem = pl.BlockSpec(memory_space=pltpu.VMEM)
    hbm = pl.BlockSpec(memory_space=pltpu.HBM)

    def call(body, slots, matmuls, outs, operands, scratch=(), places=None, lasts=(), alias=None):
        flops = 2 * matmuls * slots * BLK * lanes * size
        return pl.pallas_call(
            functools.partial(body, plan),
            in_specs=places or [vmem] * len(operands),
            out_specs=[vmem] * (len(outs) - len(lasts)) + list(lasts),
            out_shape=outs,
            scratch_shapes=list(scratch),
            input_output_aliases=alias or {},
            compiler_params=pltpu.CompilerParams(vmem_limit_bytes=20 << 20),
            cost_estimate=pl.CostEstimate(
                flops=flops, bytes_accessed=4 * queries.size, transcendentals=slots * BLK * lanes
            ),
        )(*operands)

    n_own, n_prev, n_far = plan.own_at[-1], plan.prev_at[-1], count * blocks
    stat = array(blocks, 8, lanes, dtype=F32)
    acc = array(blocks, size + 8, lanes, dtype=F32)
    total = array(rows, size, dtype=F32)
    bias = array(blocks, 16, lanes, dtype=F32)
    grads_t = array(blocks, size, lanes)
    own_shape, prev_shape = array(n_own * BLK, lanes), array(n_prev * BLK, lanes)
    ds_shape = array(blocks, count * BLK, lanes)
    far_shape = array(count, rows, size)
    full = array(*queries.shape)
    whole = pltpu.VMEM(queries.shape, BF16)

    causal = call(causal_mask, n_own, 8, [array(BLK, lanes, dtype=F32)], ())[0]
    bias, stat_own, acc_own, p_own, grad_t, query_t = call(
        local_forward, n_own, 2,
        [bias, stat, acc, own_shape, grads_t, grads_t],
        (link_mask, causal, queries, out_grad, key_rows, value_rows),
        places=[vmem] * 6,
    )
    stat_near, acc_near, p_prev = call(
        prev_forward, n_prev, 2,
        [stat, acc, prev_shape],
        (queries, k_prev, v_prev, grad_t, bias, stat_own, acc_own),
    )
    dv_far, low_far, fin = call(
        far_scores, n_far, 2,
        [far_shape, ds_shape, stat],
        (queries, grad_t, k_far, bias, stat_near, acc_near),
    )
    dk_far, ds_far, fin = call(
        far_keys, n_far, 2,
        [far_shape, ds_shape, stat],
        (query_t, grad_t, v_far, low_far, fin),
    )
    dv_prev, scaled = call(prev_values, n_prev, 1, [total, grads_t], (grad_t, fin, p_prev))
    dk_prev, ds_prev = call(prev_keys, n_prev, 2, [total, prev_shape], (query_t, v_prev, fin, p_prev, scaled))
    dk_own, dv_own, output, query_grad = call(
        local_backward, n_own, 5,
        [total, total, full, full],
        (query_t, grad_t, keys, values, k_prev, k_far, v_far, fin, acc_near, low_far, p_own, ds_prev, ds_far),
        scratch=[
            pltpu.VMEM(grads_t.shape, BF16), pltpu.VMEM(own_shape.shape, BF16), whole, whole, pltpu.SemaphoreType.DMA((2 * blocks,))
        ],
        lasts=(hbm, hbm),
    )

    def send_back(pending, prev):
        levels = [(1, prev)] + [(hop, pending[n].astype(F32)) for n, hop in enumerate(plan.hops)]
        arrived = None
        for n in reversed(range(len(levels))):
            hop, mine = levels[n]
            below = levels[n - 1][0] if n > 0 else 0
            running = mine if arrived is None else mine + arrived.astype(F32)
            arrived = shift(running.astype(BF16), "ctx", below - hop, hop)
        return arrived

    v_arrived = send_back(dv_far, dv_prev)
    k_arrived = send_back(dk_far, dk_prev)
    line = array(1, rows, size)
    key_grad, value_grad = call(
        finish, 1, 1, [line, line], (dk_own, dv_own, k_arrived, v_arrived),
        scratch=[pltpu.VMEM(line.shape, BF16), pltpu.VMEM(line.shape, BF16), pltpu.SemaphoreType.DMA((2,))],
        lasts=(hbm, hbm),
    )
    return output, query_grad, key_grad, value_grad


def solution(mesh):
    split = P(("groups", "head"), "ctx", None)

    return jax.shard_map(
        local,
        mesh=mesh,
        in_specs=(split, split, split, split, P(("groups", "ctx"), None)),
        out_specs=(split, split, split, split),
        check_vma=False,
    )
```

```python
import functools
import math

import jax
import jax.numpy as jnp
from jax import lax
from jax.experimental import pallas as pl
from jax.experimental.pallas import tpu as pltpu
from jax.sharding import PartitionSpec as P


BLK = 128
NOFF = 11
OWN_WIDE = 8
PREV_WIDE = 4
SCORE_WIDE = 2
KEY_WIDE = 4
BACK_WIDE = 2
NEG = -1e30
LOG2E = 1.4426950408889634
F32 = jnp.float32
BF16 = jnp.bfloat16


def shift(value, axis, steps, holders):
    count = lax.axis_size(axis)
    return lax.ppermute(value, axis, [(n, n + steps) for n in range(holders, count) if 0 <= n + steps < count])


def two_up(own, near, axis):
    count = lax.axis_size(axis)
    straight = lax.ppermute(own, axis, [(n, n + 2) for n in range(0, count - 2, 2)])
    relayed = lax.ppermute(near, axis, [(n, n + 1) for n in range(2, count - 1, 2)])
    return straight + relayed


def far_rows(own, near, hops):
    rows = [two_up(own, near, "ctx")]
    for at, hop in zip(hops, hops[1:]):
        rows.append(shift(rows[-1], "ctx", hop - at, at))
    return rows[0][None] if len(rows) == 1 else jnp.stack(rows)


def slot_table(block_count, ctx_size):
    entries = []
    for slot_id in range(NOFF):
        offset = 0 if slot_id == 0 else 2 ** (slot_id - 1)
        if offset < block_count:
            entries.append((slot_id, offset, 0))
        elif offset // block_count < ctx_size:
            entries.append((slot_id, offset, offset // block_count))
    return entries


def dot_nt(a, b):
    return lax.dot_general(a, b, (((1,), (1,)), ((), ())), preferred_element_type=F32)


def dot_nn(a, b):
    return lax.dot_general(a, b, (((1,), (0,)), ((), ())), preferred_element_type=F32)


def block(n):
    return slice(n * BLK, (n + 1) * BLK)


def stack(parts, axis=0):
    return parts[0] if len(parts) == 1 else jnp.concatenate(parts, axis=axis)


class Plan:
    def __init__(self, blocks, heads, size, ctx_size):
        self.blocks, self.heads, self.size = blocks, heads, size
        self.entries = slot_table(blocks, ctx_size)
        self.lanes = heads * BLK
        near = [(n, e[1]) for n, e in enumerate(self.entries) if e[1] <= blocks]
        self.far = [n for n, e in enumerate(self.entries) if e[1] > blocks]
        self.hops = [self.entries[n][2] for n in self.far]
        self.own = [[(n, i - o) for n, o in near if o <= i] for i in range(blocks)]
        self.prev = [[(n, i - o + blocks) for n, o in near if o > i] for i in range(blocks)]
        self.own_at = [sum(len(s) for s in self.own[:i]) for i in range(blocks + 1)]
        self.prev_at = [sum(len(s) for s in self.prev[:i]) for i in range(blocks + 1)]
        self.scale = LOG2E / math.sqrt(size)
        self.inv_root = 1.0 / math.sqrt(size)

    def chunks(self, wide):
        for first in range(0, self.heads, wide):
            yield slice(first, first + wide), slice(first * BLK, (first + wide) * BLK)

    def items(self, wide, rows=None):
        for i in range(self.blocks) if rows is None else rows:
            for heads, lanes in self.chunks(wide):
                yield i, heads, lanes


def rows_of(ref, heads, i, size):
    return ref[heads, block(i)].reshape(-1, size)


def with_ones(values_t):
    width = values_t.shape[1]
    row = lax.broadcasted_iota(jnp.int32, (16, width), 0)
    return jnp.concatenate([values_t, jnp.where(row == 0, 1.0, 0.0).astype(BF16)], axis=0)


def scores_of(plan, raw, biases, mask, top):
    parts = [raw[block(n)] for n in range(len(biases))]
    if mask is not None:
        parts[0] = parts[0] + mask
    for part, bias in zip(parts, biases):
        high = jnp.max(part, axis=0, keepdims=True) * plan.scale
        if bias is not None:
            high = high + bias
        top = high if top is None else jnp.maximum(top, high)
    exps = []
    for part, bias in zip(parts, biases):
        base = top if bias is None else top - bias
        exps.append(jnp.exp2(part * plan.scale - base))
    return exps, top


def staged(items, *stages):
    items = list(items)
    held = {}
    for step in range(len(items) + len(stages) - 1):
        for k, stage in enumerate(stages):
            n = step - k
            if 0 <= n < len(items):
                held[n] = stage(items[n], *held.pop(n, ()))


def causal_mask(plan, mask_ref):
    key = lax.broadcasted_iota(jnp.int32, mask_ref.shape, 0)
    row = lax.broadcasted_iota(jnp.int32, mask_ref.shape, 1)
    mask_ref[...] = jnp.where(key <= lax.rem(row, BLK), 0.0, NEG)


def local_forward(
    plan, link_ref, causal_ref, q_ref, do_ref, k_ref, v_ref, bias_ref, stat_ref, acc_ref, p_ref, dot_ref, qt_ref
):
    first_block = lax.axis_index("ctx") * plan.blocks
    for i in range(plan.blocks):
        for n, (slot_id, offset, _) in enumerate(plan.entries):
            dead = jnp.where(link_ref[i : i + 1, slot_id : slot_id + 1] == 1, 0.0, NEG).astype(F32)
            late = jnp.where(first_block + i >= offset, 0.0, NEG).astype(F32)
            bias_ref[i, n : n + 1, :] = jnp.broadcast_to(dead + late, (1, plan.lanes))
    values_t = with_ones(v_ref[0].T)
    size = plan.size

    def first(item):
        i, heads, _ = item
        keys = stack([k_ref[0, block(b)] for _, b in plan.own[i]])
        return (dot_nt(keys, rows_of(q_ref, heads, i, size)),)

    def second(item, raw):
        i, _, lanes = item
        slots = plan.own[i]
        biases = [bias_ref[i, n : n + 1, lanes] if plan.entries[n][1] > 0 else None for n, _ in slots]
        at = plan.own_at[i] * BLK
        exps, top = scores_of(plan, raw, biases, causal_ref[:, lanes], None)
        low = stack([part.astype(BF16) for part in exps])
        p_ref[at : at + low.shape[0], lanes] = low
        stat_ref[i, 0:1, lanes] = top
        return (low,)

    def third(item, low):
        i, heads, lanes = item
        vt = stack([values_t[:, block(b)] for _, b in plan.own[i]], axis=1)
        acc_ref[i, :, lanes] = dot_nn(vt, low)[: size + 8]
        dot_ref[i, :, lanes] = rows_of(do_ref, heads, i, size).T
        qt_ref[i, :, lanes] = rows_of(q_ref, heads, i, size).T
        return ()

    staged(plan.items(OWN_WIDE), first, second, third)


def prev_forward(plan, q_ref, k_ref, v_ref, dot_ref, bias_ref, stat_in, acc_in, stat_ref, acc_ref, p_ref):
    size = plan.size
    values_t = with_ones(v_ref[...].T)

    def first(item):
        i, heads, _ = item
        keys = stack([k_ref[block(b)] for _, b in plan.prev[i]])
        return (dot_nt(keys, rows_of(q_ref, heads, i, size)),)

    def second(item, raw):
        i, _, lanes = item
        slots = plan.prev[i]
        at = plan.prev_at[i] * BLK
        before = stat_in[i, 0:1, lanes]
        biases = [bias_ref[i, n : n + 1, lanes] for n, _ in slots]
        exps, top = scores_of(plan, raw, biases, None, before)
        low = stack([part.astype(BF16) for part in exps])
        p_ref[at : at + low.shape[0], lanes] = low
        return low, before, top

    def third(item, low, before, top):
        i, _, lanes = item
        vt = stack([values_t[:, block(b)] for _, b in plan.prev[i]], axis=1)
        acc = acc_in[i, :, lanes] * jnp.exp2(before - top) + dot_nn(vt, low)[: size + 8]
        acc_ref[i, :, lanes] = acc
        stat_ref[i, 0:1, lanes] = before
        stat_ref[i, 1:2, lanes] = top
        stat_ref[i, 2:3, lanes] = jnp.sum(acc[:size] * dot_ref[i, :, lanes].astype(F32), axis=0, keepdims=True)
        return ()

    staged(plan.items(PREV_WIDE), first, second, third)


def has_far(plan):
    return (lax.axis_index("ctx") + 1) * plan.blocks > plan.entries[plan.far[0]][1]


def far_scores(plan, q_ref, dot_ref, k_ref, bias_ref, stat_ref, acc_ref, dv_ref, low_ref, fin_ref):
    size = plan.size
    count = len(plan.far)

    def first(item):
        i, heads, _ = item
        keys = stack([k_ref[f, block(i)] for f in range(count)])
        return (dot_nt(keys, rows_of(q_ref, heads, i, size)),)

    def second(item, raw):
        i, _, lanes = item
        before = stat_ref[i, 1:2, lanes]
        biases = [bias_ref[i, n : n + 1, lanes] for n in plan.far]
        exps, top = scores_of(plan, raw, biases, None, before)
        fade = jnp.exp2(before - top)
        total = acc_ref[i, size : size + 1, lanes] * fade
        total = total + sum(jnp.sum(part, axis=0, keepdims=True) for part in exps)
        inverse = 1.0 / total
        low_ref[i, :, lanes] = (stack(exps) * inverse).astype(BF16)
        fin_ref[i, 0:1, lanes] = jnp.exp2(stat_ref[i, 0:1, lanes] - top) * inverse
        fin_ref[i, 1:2, lanes] = fade * inverse
        fin_ref[i, 2:3, lanes] = stat_ref[i, 2:3, lanes] * (fade * inverse)
        return ()

    def third(item):
        i, _, lanes = item
        if lanes.stop == plan.lanes:
            dv = dot_nt(low_ref[i], dot_ref[i])
            for f in range(count):
                dv_ref[f, block(i)] = dv[block(f)].astype(BF16)
        return ()

    @pl.when(has_far(plan))
    def _():
        staged(plan.items(SCORE_WIDE), first, second, third)

    @pl.when(jnp.logical_not(has_far(plan)))
    def _():
        dv_ref[...] = jnp.zeros_like(dv_ref)
        low_ref[...] = jnp.zeros_like(low_ref)
        for i in range(plan.blocks):
            inverse = 1.0 / acc_ref[i, size : size + 1, :]
            fin_ref[i, 0:1, :] = jnp.exp2(stat_ref[i, 0:1, :] - stat_ref[i, 1:2, :]) * inverse
            fin_ref[i, 1:2, :] = inverse
            fin_ref[i, 2:3, :] = stat_ref[i, 2:3, :] * inverse


def far_keys(plan, qt_ref, dot_ref, v_ref, low_ref, fin_in, dk_ref, ds_ref, fin_ref):
    count = len(plan.far)

    def first(item):
        i, _, lanes = item
        values = stack([v_ref[f, block(i)] for f in range(count)])
        return (dot_nn(values, dot_ref[i, :, lanes]),)

    def second(item, grad_w):
        i, _, lanes = item
        weights = low_ref[i, :, lanes].astype(F32)
        products = weights * grad_w
        row_dot = fin_in[i, 2:3, lanes] + jnp.sum(products, axis=0, keepdims=True)
        ds_ref[i, :, lanes] = (products - weights * row_dot).astype(BF16)
        fin_ref[i, 2:3, lanes] = row_dot
        return ()

    def third(item):
        i, _, lanes = item
        if lanes.stop == plan.lanes:
            dk = dot_nt(ds_ref[i], qt_ref[i]) * plan.inv_root
            for f in range(count):
                dk_ref[f, block(i)] = dk[block(f)].astype(BF16)
        return ()

    fin_ref[...] = fin_in[...]

    @pl.when(has_far(plan))
    def _():
        staged(plan.items(KEY_WIDE), first, second, third)

    @pl.when(jnp.logical_not(has_far(plan)))
    def _():
        dk_ref[...] = jnp.zeros_like(dk_ref)
        ds_ref[...] = jnp.zeros_like(ds_ref)


def add_blocks(sums, slots, parts):
    for n, (_, b) in enumerate(slots):
        part = parts[block(n)]
        sums[b] = part if b not in sums else sums[b] + part


def scale_rows(plan, i, factor, dot_ref, fin_ref, scaled_ref):
    for heads, lanes in plan.chunks(BACK_WIDE):
        fade = fin_ref[i, factor : factor + 1, lanes]
        scaled_ref[i, :, lanes] = (dot_ref[i, :, lanes].astype(F32) * fade).astype(BF16)


def score_grads(plan, i, slots, values, factor, fin_ref, p_ref, p_at, ds_ref, ds_at, scaled_ref):
    tall = len(slots) * BLK
    for heads, lanes in plan.chunks(BACK_WIDE):
        fade = fin_ref[i, factor : factor + 1, lanes]
        shifted = dot_nn(values, scaled_ref[i, :, lanes]) - fin_ref[i, 2:3, lanes] * fade
        ds_ref[ds_at : ds_at + tall, lanes] = (p_ref[p_at : p_at + tall, lanes].astype(F32) * shifted).astype(BF16)


def prev_backward(
    plan, qt_ref, dot_ref, v_ref, vf_ref, fin_ref, acc_ref, low_ref, p_ref, dk_ref, dv_ref, ds_ref, o_hbm, scaled_ref, o_ref, sems
):
    size = plan.size
    copies = []
    for i in range(plan.blocks):
        vt = stack([vf_ref[f, block(i)] for f in range(len(plan.far))]).T
        for heads, lanes in plan.chunks(BACK_WIDE):
            out_t = acc_ref[i, :size, lanes] * fin_ref[i, 1:2, lanes] + dot_nn(vt, low_ref[i, :, lanes])
            o_ref[heads, block(i)] = out_t.astype(BF16).T.reshape(BACK_WIDE, BLK, size)
        copies.append(pltpu.make_async_copy(o_ref.at[:, block(i)], o_hbm.at[:, block(i)], sems.at[i]))
        copies[i].start()
    dk_sums, dv_sums = {}, {}
    for i in range(plan.blocks):
        slots = plan.prev[i]
        values = stack([v_ref[block(b)] for _, b in slots])
        at, end = plan.prev_at[i] * BLK, plan.prev_at[i + 1] * BLK
        scale_rows(plan, i, 1, dot_ref, fin_ref, scaled_ref)
        score_grads(plan, i, slots, values, 1, fin_ref, p_ref, at, ds_ref, at, scaled_ref)
        add_blocks(dv_sums, slots, dot_nt(p_ref[at:end, :], scaled_ref[i]))
        add_blocks(dk_sums, slots, dot_nt(ds_ref[at:end, :], qt_ref[i]))
    for b in range(plan.blocks):
        dk_ref[block(b)] = dk_sums[b] * plan.inv_root
        dv_ref[block(b)] = dv_sums[b]
    for copy in copies:
        copy.wait()


def local_backward(
    plan, qt_ref, dot_ref, k_ref, v_ref, kp_ref, kf_ref, fin_ref, p_ref, dsp_ref, dsf_ref,
    dk_ref, dv_ref, dq_hbm, scaled_ref, ds_ref, dq_ref, sems,
):
    size = plan.size
    count = len(plan.far)
    copies = []

    def send(source, target, i):
        copies.append(pltpu.make_async_copy(source.at[:, block(i)], target.at[:, block(i)], sems.at[len(copies)]))
        copies[-1].start()

    dk_sums, dv_sums = {}, {}
    keys_t = k_ref[...].T
    prev_t = kp_ref[...].T
    for i in range(plan.blocks):
        slots = plan.own[i]
        values = stack([v_ref[block(b)] for _, b in slots])
        at, end = plan.own_at[i] * BLK, plan.own_at[i + 1] * BLK
        scale_rows(plan, i, 0, dot_ref, fin_ref, scaled_ref)
        score_grads(plan, i, slots, values, 0, fin_ref, p_ref, at, ds_ref, at, scaled_ref)
        kt = [keys_t[:, block(b)] for _, b in slots]
        kt += [prev_t[:, block(b)] for _, b in plan.prev[i]]
        kt += [kf_ref[f, block(i)].T for f in range(count)]
        kt = stack(kt, axis=1)
        for heads, lanes in plan.chunks(BACK_WIDE):
            ds = [ds_ref[at:end, lanes]]
            if plan.prev[i]:
                ds.append(dsp_ref[plan.prev_at[i] * BLK : plan.prev_at[i + 1] * BLK, lanes])
            if count:
                ds.append(dsf_ref[i, :, lanes])
            dq_t = (dot_nn(kt, stack(ds)) * plan.inv_root).astype(BF16)
            dq_ref[heads, block(i)] = dq_t.T.reshape(BACK_WIDE, BLK, size)
        send(dq_ref, dq_hbm, i)
    for i in range(plan.blocks):
        at, end = plan.own_at[i] * BLK, plan.own_at[i + 1] * BLK
        add_blocks(dv_sums, plan.own[i], dot_nt(p_ref[at:end, :], scaled_ref[i]))
        add_blocks(dk_sums, plan.own[i], dot_nt(ds_ref[at:end, :], qt_ref[i]))
    for b in range(plan.blocks):
        dk_ref[block(b)] = dk_sums[b] * plan.inv_root
        dv_ref[block(b)] = dv_sums[b]
    for copy in copies:
        copy.wait()


def finish(plan, own_ref, arrived_ref, target_hbm, out, sem):
    out[0] = (own_ref[...] + arrived_ref[...].astype(F32)).astype(BF16)
    copy = pltpu.make_async_copy(out, target_hbm, sem.at[0])
    copy.start()
    copy.wait()


def local(queries, key_rows, value_rows, out_grad, link_mask):
    heads, rows, size = queries.shape
    blocks = rows // BLK
    plan = Plan(blocks, heads, size, lax.axis_size("ctx"))
    lanes = plan.lanes
    count = len(plan.far)

    keys, values = key_rows[0], value_rows[0]
    k_prev = shift(keys, "ctx", 1, 0)
    v_prev = shift(values, "ctx", 1, 0)
    k_far = far_rows(keys, k_prev, plan.hops)
    v_far = far_rows(values, v_prev, plan.hops)

    def array(*shape, dtype=BF16):
        return jax.ShapeDtypeStruct(shape, dtype)

    vmem = pl.BlockSpec(memory_space=pltpu.VMEM)
    hbm = pl.BlockSpec(memory_space=pltpu.HBM)

    def call(body, slots, matmuls, outs, operands, scratch=(), places=None, lasts=(), alias=None):
        flops = 2 * matmuls * slots * BLK * lanes * size
        return pl.pallas_call(
            functools.partial(body, plan),
            in_specs=places or [vmem] * len(operands),
            out_specs=[vmem] * (len(outs) - len(lasts)) + list(lasts),
            out_shape=outs,
            scratch_shapes=list(scratch),
            input_output_aliases=alias or {},
            compiler_params=pltpu.CompilerParams(vmem_limit_bytes=20 << 20),
            cost_estimate=pl.CostEstimate(
                flops=flops, bytes_accessed=4 * queries.size, transcendentals=slots * BLK * lanes
            ),
        )(*operands)

    n_own, n_prev, n_far = plan.own_at[-1], plan.prev_at[-1], count * blocks
    stat = array(blocks, 8, lanes, dtype=F32)
    acc = array(blocks, size + 8, lanes, dtype=F32)
    total = array(rows, size, dtype=F32)
    bias = array(blocks, 16, lanes, dtype=F32)
    grads_t = array(blocks, size, lanes)
    own_shape, prev_shape = array(n_own * BLK, lanes), array(n_prev * BLK, lanes)
    ds_shape = array(blocks, count * BLK, lanes)
    far_shape = array(count, rows, size)
    full = array(*queries.shape)
    whole = pltpu.VMEM(queries.shape, BF16)

    causal = call(causal_mask, n_own, 8, [array(BLK, lanes, dtype=F32)], ())[0]
    bias, stat_own, acc_own, p_own, grad_t, query_t = call(
        local_forward, n_own, 2,
        [bias, stat, acc, own_shape, grads_t, grads_t],
        (link_mask, causal, queries, out_grad, key_rows, value_rows),
        places=[vmem] * 6,
    )
    stat_near, acc_near, p_prev = call(
        prev_forward, n_prev, 2,
        [stat, acc, prev_shape],
        (queries, k_prev, v_prev, grad_t, bias, stat_own, acc_own),
    )
    dv_far, low_far, fin = call(
        far_scores, n_far, 2,
        [far_shape, ds_shape, stat],
        (queries, grad_t, k_far, bias, stat_near, acc_near),
    )
    dk_far, ds_far, fin = call(
        far_keys, n_far, 2,
        [far_shape, ds_shape, stat],
        (query_t, grad_t, v_far, low_far, fin),
    )
    dk_prev, dv_prev, ds_prev, output = call(
        prev_backward, n_prev, 4,
        [total, total, prev_shape, full],
        (query_t, grad_t, v_prev, v_far, fin, acc_near, low_far, p_prev),
        scratch=[pltpu.VMEM(grads_t.shape, BF16), whole, pltpu.SemaphoreType.DMA((blocks,))],
        lasts=(hbm,),
    )
    dk_own, dv_own, query_grad = call(
        local_backward, n_own, 5,
        [total, total, full],
        (query_t, grad_t, keys, values, k_prev, k_far, fin, p_own, ds_prev, ds_far),
        scratch=[
            pltpu.VMEM(grads_t.shape, BF16), pltpu.VMEM(own_shape.shape, BF16), whole, pltpu.SemaphoreType.DMA((blocks,))
        ],
        lasts=(hbm,),
    )

    def send_back(pending, prev):
        levels = [(1, prev)] + [(hop, pending[n].astype(F32)) for n, hop in enumerate(plan.hops)]
        arrived = None
        for n in reversed(range(len(levels))):
            hop, mine = levels[n]
            below = levels[n - 1][0] if n > 0 else 0
            running = mine if arrived is None else mine + arrived.astype(F32)
            arrived = shift(running.astype(BF16), "ctx", below - hop, hop)
        return arrived

    v_arrived = send_back(dv_far, dv_prev)
    k_arrived = send_back(dk_far, dk_prev)
    line = array(1, rows, size)
    value_grad, key_grad = (
        call(
            finish, 1, 1, [line], pair,
            scratch=[pltpu.VMEM(line.shape, BF16), pltpu.SemaphoreType.DMA((1,))], lasts=(hbm,),
        )[0]
        for pair in ((dv_own, v_arrived), (dk_own, k_arrived))
    )
    return output, query_grad, key_grad, value_grad


def solution(mesh):
    split = P(("groups", "head"), "ctx", None)

    return jax.shard_map(
        local,
        mesh=mesh,
        in_specs=(split, split, split, split, P(("groups", "ctx"), None)),
        out_specs=(split, split, split, split),
        check_vma=False,
    )
```
